512 devices in a mesh: tile: 32 (over x, y, core), depth: 16 (over z).
Axes of the slice: x: 4, y: 4, z: 16, core: 2. Of those that a mesh axis runs over, the one named last changes fastest.
Arguments:
- estimate: float32 [32, 1024, 1024], P('depth', 'tile'), may hold values from 0.25 to 4
- views: bfloat16 [8, 32, 1024, 1024], P(None, 'depth', 'tile'), may hold values from 0.19921875 to 5
- kernel_x: float32 [8, 31], replicated, may hold values from 0.01 to 1
- kernel_y: float32 [8, 31], replicated, may hold values from 0.01 to 1
- kernel_z: float32 [8, 31], replicated, may hold values from 0.01 to 1
- offsets: int32 [8], replicated, may hold values from 16 to 384
Outputs:
- updated: float32 [32, 1024, 1024], P('depth', 'tile')
The draws below stay inside these ranges and needn't reach their ends.
All inputs are finite; a program needn't handle non-finite values.
Results may differ from the reference program's by a relative error of at most 0.0007.
Values may be sent and summed in bfloat16 or wider, within the bound.
A program may use at most 128 MiB of HBM per device.

```python
import math
import jax
import jax.numpy as jnp
from jax import lax

XT = 32
NY = 1024
VIEWS = 8
TAPS = 31
NZ = 32
NX = 1024
VX = 640


def set_ends(result, own_key, least, top_value):
    longest = result.shape.index(max(result.shape))
    spots = []
    for shift in (0, 1):
        where = [jax.random.randint(jax.random.fold_in(own_key, axis), (), 0, length) for axis, length in enumerate(result.shape)]
        where[longest] = (where[longest] + shift) % result.shape[longest]
        spots.append(tuple(where))
    return result.at[spots[0]].set(least).at[spots[1]].set(top_value)


def levels(own_key, shape, cuts, least, high):
    gain, own = 1.0, jax.random.fold_in(own_key, 6)
    for dim, shards_of in cuts:
        heights = jnp.exp(jax.random.uniform(jax.random.fold_in(own, dim), (shards_of,), jnp.float32, least / len(cuts), high / len(cuts)))
        gain = gain * jnp.repeat(heights, shape[dim] // shards_of).reshape([-1 if axis == dim else 1 for axis in range(len(shape))])
    return gain


def setup_inputs(seed: int = 0) -> dict:
    arg_keys = jax.random.split(jax.random.key(seed), 7)
    return {
        "estimate": jnp.clip(jnp.exp(math.log(4.0) - 2.7725887 * jax.random.uniform(arg_keys[0], (NZ, NX, NY), jnp.float32) ** levels(arg_keys[0], (NZ, NX, NY), ((0, 16), (1, 32)), -0.2, 0.2)), 0.25, 4.0),
        "views": jnp.clip(jnp.exp(math.log(5.0) - 3.2227897 * jax.random.uniform(arg_keys[1], (VIEWS, NZ, NX, NY), jnp.float32) ** levels(arg_keys[1], (VIEWS, NZ, NX, NY), ((1, 16), (2, 32)), -0.2, 0.2)), 0.19921875, 5.0).astype(jnp.bfloat16),
        "kernel_x": jnp.clip(jnp.exp(jax.random.uniform(arg_keys[2], (VIEWS, TAPS), jnp.float32, math.log(0.01), math.log(1.0))), 0.01, 1.0),
        "kernel_y": jnp.clip(jnp.exp(jax.random.uniform(arg_keys[3], (VIEWS, TAPS), jnp.float32, math.log(0.01), math.log(1.0))), 0.01, 1.0),
        "kernel_z": jnp.clip(jnp.exp(jax.random.uniform(arg_keys[4], (VIEWS, TAPS), jnp.float32, math.log(0.01), math.log(1.0))), 0.01, 1.0),
        "offsets": set_ends(jax.random.randint(arg_keys[5], (VIEWS,), XT // 2, NX - VX + 1), jax.random.fold_in(arg_keys[5], 1), XT // 2, NX - VX).astype(jnp.int32),
    }


def normalize(kernel):
    return kernel / jnp.sum(kernel, axis=1, keepdims=True)


def convolve(values, kernel, axis):
    margin = kernel.shape[0] // 2
    length = values.shape[axis]
    widths = [(0, 0)] * values.ndim
    widths[axis] = (margin, margin)
    padded = jnp.pad(values, widths)
    summed = jnp.zeros_like(values)
    for tap_index in range(kernel.shape[0]):
        summed = summed + kernel[tap_index] * lax.slice_in_dim(padded, tap_index, tap_index + length, axis=axis)
    return summed


def reference(estimate, views, kernel_x, kernel_y, kernel_z, offsets):
    kernel_x = normalize(kernel_x)
    kernel_y = normalize(kernel_y)
    kernel_z = normalize(kernel_z)
    row_ids = jnp.arange(NX, dtype=jnp.int32)
    covered = ((row_ids[None, :] >= offsets[:, None]) & (row_ids[None, :] < offsets[:, None] + VX)).astype(jnp.float32)
    coverage = jnp.sum(covered, axis=0)

    def per_view(view_index, accumulated):
        blurred = convolve(estimate, kernel_x[view_index], 1)
        blurred = convolve(blurred, kernel_y[view_index], 2)
        blurred = convolve(blurred, kernel_z[view_index], 0)
        recorded = views[view_index].astype(jnp.float32)
        correction = covered[view_index][None, :, None] * (recorded / blurred - 1.0)
        backward = convolve(correction, kernel_z[view_index][::-1], 0)
        backward = convolve(backward, kernel_y[view_index][::-1], 2)
        backward = convolve(backward, kernel_x[view_index][::-1], 1)
        return accumulated + backward

    summed = lax.fori_loop(0, VIEWS, per_view, jnp.zeros_like(estimate))
    return estimate * (1.0 + summed / jnp.maximum(coverage, 1.0)[None, :, None])
```

```python
import jax
import jax.numpy as jnp
from jax import lax
from jax.experimental import pallas as pl
from jax.experimental.pallas import tpu as pltpu
from jax.sharding import PartitionSpec as P

MESH = pl.DeviceIdType.MESH
BF = jnp.bfloat16
F32 = jnp.float32
V = 8
T = 31
R = 32
H = 16
RH = R + 2 * H
NC = 1024
PAD = 128
CT = 256


def place(way, hop):
    if hop == 0:
        return 0, 0
    if hop == 8:
        return 0, 1
    return hop, way


def body(
    est, views, kx, ky, kz, offs, out,
    gath, acc, blur, corr, back, amat, bmat, xfwd, xbwd, yfwd, ybwd, vbuf, part, own, sbuf, rbuf,
    g_send, g_recv, h_send, h_recv, v_sem, y_send, y_recv, r_send, r_recv,
):
    b = lax.axis_index("depth")
    t = lax.axis_index("tile")
    nz = lax.axis_size("depth")
    nt = lax.axis_size("tile")
    rows_total = R * nt
    view_rows = 5 * rows_total // 8
    zr = lax.rem(b + 1, nz)
    zl = lax.rem(b + nz - 1, nz)
    tu = lax.rem(t + nt - 1, nt)
    td = lax.rem(t + 1, nt)
    z_to = ((t, zr), (t, zl))
    t_to = ((tu, b), (td, b))

    barrier = pltpu.get_barrier_semaphore()
    corners = tuple((x, z) for x in (tu, td) for z in (zr, zl))
    for device in z_to + t_to + corners:
        pl.semaphore_signal(barrier, inc=1, device_id=device, device_id_type=MESH)
    vcopy = pltpu.make_async_copy(views, vbuf, v_sem)
    vcopy.start()
    gath[0, 0, :, H : H + R, :] = est[...].astype(BF)

    def hop_copy(way, hop, q, k):
        pair, side = place(way, hop)
        pair2, side2 = place(way, hop + 1)
        return pltpu.make_async_remote_copy(
            src_ref=gath.at[pair, side, q, pl.ds(H + k * H, H), :],
            dst_ref=gath.at[pair2, side2, q, pl.ds(H + k * H, H), :],
            send_sem=g_send.at[way, hop, q, k],
            recv_sem=g_recv.at[way, hop, q, k],
            device_id=z_to[way],
            device_id_type=MESH,
        )

    def halo_copy(pair, side, q, k):
        src, dst = ((H, H + R), (R, 0))[k]
        pair2, side2, device = pair, side, t_to[k]
        if (pair, side) == (0, 1):
            way = 1 - q
            pair2, side2 = place(way, 7)
            device = ((tu, td)[k], (zr, zl)[way])
        return pltpu.make_async_remote_copy(
            src_ref=gath.at[pair2, side2, q, pl.ds(src, H), :],
            dst_ref=gath.at[pair, side, q, pl.ds(dst, H), :],
            send_sem=h_send.at[pair, side, q, k],
            recv_sem=h_recv.at[pair, side, q, k],
            device_id=device,
            device_id_type=MESH,
        )

    pl.semaphore_wait(barrier, 8)
    planes = ((1, 0), (0, 1))
    pieces = ((0, 0), (0, 1), (1, 0), (1, 1))
    for i, k in pieces:
        for way in range(2):
            hop_copy(way, 0, planes[way][i], k).start()
    for q in range(2):
        for k in range(2):
            halo_copy(0, 0, q, k).start()

    lane = lax.broadcasted_iota(jnp.int32, (R, 2 * RH), 1)
    low = lane < RH
    src_row = jnp.where(low, lane, lane - RH)
    diff = src_row - lax.broadcasted_iota(jnp.int32, (R, 2 * RH), 0) - 1
    row_at = src_row + (t * R - H)
    exists = (row_at >= 0) & (row_at < rows_total)
    gap = lax.broadcasted_iota(jnp.int32, (PAD, PAD), 0) - lax.broadcasted_iota(jnp.int32, (PAD, PAD), 1)
    ring = jnp.where(gap + 15 < 0, gap + 15 + PAD, jnp.where(gap + 15 >= PAD, gap + 15 - PAD, gap + 15))

    def tables(v, carry):
        sx = kx[v, 0]
        sy = ky[v, 0]
        sz = kz[v, 0]
        for j in range(1, T):
            sx = sx + kx[v, j]
            sy = sy + ky[v, j]
            sz = sz + kz[v, j]
        xf = jnp.zeros((R, 2 * RH), F32)
        xb = jnp.zeros((R, 2 * RH), F32)
        cf = jnp.zeros((PAD, PAD), F32)
        cb = jnp.zeros((PAD, PAD), F32)
        for j in range(T):
            hit = diff == j
            xf = jnp.where(hit, kx[v, j], xf)
            xb = jnp.where(hit, kx[v, T - 1 - j], xb)
            hit = ring == j
            cf = jnp.where(hit, ky[v, j], cf)
            cb = jnp.where(hit, ky[v, T - 1 - j], cb)
        scale = jnp.full((R, 2 * RH), sx * sz, F32)
        xfwd[v] = jnp.where(exists, xf / scale, 0.0)
        xbwd[v] = jnp.where(exists, xb / scale, 0.0)
        for ref, c in ((yfwd, cf), (ybwd, cb)):
            c = c / jnp.full((PAD, PAD), sy, F32)
            bands = (
                jnp.where(gap >= PAD - 15, c, 0.0).astype(BF),
                jnp.where((gap <= 15) & (gap >= -15), c, 0.0).astype(BF),
                jnp.where(gap <= 15 - PAD, c, 0.0).astype(BF),
            )
            none = jnp.zeros((PAD, PAD), BF)
            for i in range(4):
                for j in range(2):
                    ref[v, PAD * i : PAD * (i + 1), PAD * j : PAD * (j + 1)] = bands[i - j] if 0 <= i - j < 3 else none
        return carry

    lax.fori_loop(0, V, tables, 0)

    def mats(pair):
        offsets = (0, 8) if pair == 0 else (-pair, pair)
        zs = [2 * lax.rem(b + o + nz, nz) - 2 * b + 15 for o in offsets]

        def one(v, carry):
            xf = xfwd[v]
            xb = xbwd[v]
            c = {}
            for side in range(2):
                for q in range(2):
                    for p in range(2):
                        at = zs[side] + (q - p)
                        ok = (at >= 0) & (at < T)
                        c[side, q, p] = jnp.where(ok, kz[v, jnp.clip(at, 0, T - 1)], 0.0)
            for side in range(2):
                for p in range(2):
                    z = jnp.where(low, c[side, 0, p], c[side, 1, p])
                    amat[pair, pl.ds(pl.multiple_of(v * 64 + p * R, R), R), side * 128 : side * 128 + 128] = (xf * z).astype(BF)
                for q in range(2):
                    z = jnp.where(low, c[side, q, 0], c[side, q, 1])
                    first = side * 64 + q * R
                    bmat[pair, first : first + R, pl.ds(pl.multiple_of(v * 128, 128), 128)] = (xb * z).astype(BF)
            return carry

        lax.fori_loop(0, V, one, 0)

    def forward(pair, begin, end):
        def one(n, carry):
            cols = pl.ds(pl.multiple_of(n * CT, CT), CT)
            block = gath[pair, :, :, :, cols].reshape(4 * RH, CT)
            got = jnp.dot(amat[pair], block, preferred_element_type=F32)
            if not begin:
                got = got + acc[:, cols]
            if end:
                blur[:, pl.ds(pl.multiple_of(n * CT + PAD, PAD), CT)] = got.astype(BF)
            else:
                acc[:, cols] = got
            return carry

        lax.fori_loop(0, NC // CT, one, 0)

    for ref in (blur, corr):
        ref[:, :PAD] = jnp.zeros((ref.shape[0], PAD), BF)
        ref[:, PAD + NC :] = jnp.zeros((ref.shape[0], PAD), BF)

    def halos(pair, side):
        for q in range(2):
            for k in range(2):
                halo_copy(pair, side, q, k).wait_recv()

    for hop in range(1, 8):
        for i, k in pieces:
            for way in range(2):
                q = planes[way][i]
                hop_copy(way, hop - 1, q, k).wait_recv()
                if hop < 7 or i == 0:
                    hop_copy(way, hop, q, k).start()
                if hop == 7 and i == 0:
                    halo_copy(0, 1, q, k).start()
        for side in range(2):
            for q in range(2):
                for k in range(2):
                    halo_copy(hop, side, q, k).start()
        mats(hop)
        if hop >= 2:
            for side in range(2):
                halos(hop - 1, side)
            forward(hop - 1, hop == 2, False)
    mats(0)
    for side in range(2):
        halos(7, side)
    forward(7, False, False)
    for k in range(2):
        for way in range(2):
            hop_copy(way, 7, planes[way][0], k).wait_recv()
    for side in range(2):
        halos(0, side)
    forward(0, False, True)
    vcopy.wait()

    row = lax.broadcasted_iota(jnp.int32, (2 * R, CT), 0)
    row = jnp.where(row >= R, row - R, row) + t * R

    def y_copy(v, k):
        src, dst = ((H, H + R), (R, 0))[k]
        return pltpu.make_async_remote_copy(
            src_ref=back.at[v, :, pl.ds(src, H), :],
            dst_ref=back.at[v, :, pl.ds(dst, H), :],
            send_sem=y_send.at[v, k],
            recv_sem=y_recv.at[v, k],
            device_id=t_to[k],
            device_id_type=MESH,
        )

    def view_step(v, carry):
        inside = (row >= offs[v]) & (row < offs[v] + view_rows)
        rows = pl.ds(pl.multiple_of(v * 64, 64), 64)
        lhs = jnp.concatenate([blur[rows, n * CT : n * CT + 2 * CT] for n in range(4)], axis=0)
        blurred = jnp.dot(lhs, yfwd[v], preferred_element_type=F32)
        for n in range(4):
            seen = vbuf[v, :, :, n * CT : (n + 1) * CT].astype(F32).reshape(2 * R, CT)
            ratio = seen / blurred[n * 64 : (n + 1) * 64]
            corr[:, PAD + n * CT : PAD + (n + 1) * CT] = jnp.where(inside, ratio - 1.0, 0.0).astype(BF)
        lhs = jnp.concatenate([corr[:, n * CT : n * CT + 2 * CT] for n in range(4)], axis=0)
        spread = jnp.dot(lhs, ybwd[v], preferred_element_type=F32).astype(BF)
        for n in range(4):
            back[v, :, H : H + R, n * CT : (n + 1) * CT] = spread[n * 64 : (n + 1) * 64].reshape(2, R, CT)
        for k in range(2):
            y_copy(v, k).start()
        return carry

    lax.fori_loop(0, V, view_step, 0)

    def y_wait(v, carry):
        for k in range(2):
            y_copy(v, k).wait_recv()
        return carry

    def sum_copy(way, step, piece):
        tiles = pl.ds(0 if piece == 0 else 1 + 8 * piece, 9 if piece == 0 else 8)
        return pltpu.make_async_remote_copy(
            src_ref=sbuf.at[way, step, tiles],
            dst_ref=rbuf.at[way, step, tiles],
            send_sem=r_send.at[way, step, piece],
            recv_sem=r_recv.at[way, step, piece],
            device_id=z_to[way],
            device_id_type=MESH,
        )

    early = 6

    def project(pair, target, first, last):
        def one(n, carry):
            cols = pl.ds(pl.multiple_of(n * CT, CT), CT)
            block = back[first:last, :, :, cols].reshape((last - first) * 2 * RH, CT)
            got = jnp.dot(bmat[pair, :, first * 128 : last * 128], block, preferred_element_type=F32)
            if first:
                got = got + target[:, cols]
            target[:, cols] = got
            return carry

        lax.fori_loop(0, NC // CT, one, 0)

    def message(source, way, step, piece, plane_order):
        i, k = pieces[piece]
        q = plane_order[i]
        at = (64 if step == 0 else (1 - way) * 64) + q * R + k * H
        tiles = [source[at : at + H, 128 * j : 128 * (j + 1)] for j in range(8)]
        if step > 1 or (step == 1 and i == 0):
            sum_copy(way, step - 1, piece).wait_recv()
            base = rbuf[way, step - 1, 0].astype(F32)
            tiles = [tiles[j] + (rbuf[way, step - 1, 1 + 8 * piece + j].astype(F32) + base) for j in range(8)]
        if piece == 0:
            mean = sum(tiles[1:], tiles[0]) * 0.125
            sbuf[way, step, 0] = mean.astype(BF)
        mean = sbuf[way, step, 0].astype(F32)
        for j in range(8):
            sbuf[way, step, 1 + 8 * piece + j] = (tiles[j] - mean).astype(BF)
        sum_copy(way, step, piece).start()

    orders = ((0, 1), (1, 0))
    lax.fori_loop(0, early, y_wait, 0)
    project(0, own, 0, early)
    project(7, part, 0, early)
    lax.fori_loop(early, V, y_wait, 0)
    project(0, own, early, V)
    for piece in range(2):
        for way in range(2):
            message(own, way, 0, piece, orders[way])
    for step in range(1, 8):
        if step == 1:
            project(7, part, early, V)
        else:
            project(8 - step, part, 0, V)
        for piece in range(4):
            for way in range(2):
                message(part, way, step, piece, orders[way])
    rid = lax.broadcasted_iota(jnp.int32, (R, 128), 0) + t * R
    seen_by = jnp.zeros((R, 128), F32)
    for v in range(V):
        seen_by = seen_by + jnp.where((rid >= offs[v]) & (rid < offs[v] + view_rows), 1.0, 0.0)
    share = 1.0 / jnp.maximum(seen_by, 1.0)
    for piece in range(4):
        i, k = pieces[piece]
        for way in range(2):
            sum_copy(way, 7, piece).wait_recv()
            q = orders[way][i]
            base = rbuf[way, 7, 0].astype(F32)
            for j in range(8):
                at = (q * R + k * H, q * R + (k + 1) * H)
                cols = slice(128 * j, 128 * (j + 1))
                own[at[0] : at[1], cols] = own[at[0] : at[1], cols] + (rbuf[way, 7, 1 + 8 * piece + j].astype(F32) + base)
    for q in range(2):
        for j in range(8):
            cols = slice(128 * j, 128 * (j + 1))
            out[q, :, cols] = est[q, :, cols] * (1.0 + own[q * R : (q + 1) * R, cols] * share)

    for hop in range(8):
        for way in range(2):
            for piece in range(4):
                i, k = pieces[piece]
                if hop < 7 or i == 0:
                    hop_copy(way, hop, planes[way][i], k).wait_send()
                if hop > 0 or i == 0:
                    sum_copy(way, hop, piece).wait_send()
        for side in range(2):
            for q in range(2):
                for k in range(2):
                    halo_copy(hop, side, q, k).wait_send()
    for v in range(V):
        for k in range(2):
            y_copy(v, k).wait_send()


def shards(estimate, views, kernel_x, kernel_y, kernel_z, offsets):
    smem = pl.BlockSpec(memory_space=pltpu.SMEM)
    vmem = pl.BlockSpec(memory_space=pltpu.VMEM)
    dma = pltpu.SemaphoreType.DMA
    return pl.pallas_call(
        body,
        out_shape=jax.ShapeDtypeStruct(estimate.shape, F32),
        in_specs=[vmem, pl.BlockSpec(memory_space=pl.ANY), smem, smem, smem, smem],
        out_specs=vmem,
        scratch_shapes=[
            pltpu.VMEM((8, 2, 2, RH, NC), BF),
            pltpu.VMEM((V * 64, NC), F32),
            pltpu.VMEM((V * 64, NC + 2 * PAD), BF),
            pltpu.VMEM((64, NC + 2 * PAD), BF),
            pltpu.VMEM((V, 2, RH, NC), BF),
            pltpu.VMEM((8, V * 64, 256), BF),
            pltpu.VMEM((8, 128, V * 128), BF),
            pltpu.VMEM((V, R, 128), F32),
            pltpu.VMEM((V, R, 128), F32),
            pltpu.VMEM((V, 512, 256), BF),
            pltpu.VMEM((V, 512, 256), BF),
            pltpu.VMEM((V, 2, R, NC), BF),
            pltpu.VMEM((128, NC), F32),
            pltpu.VMEM((128, NC), F32),
            pltpu.VMEM((2, 8, 33, H, 128), BF),
            pltpu.VMEM((2, 8, 33, H, 128), BF),
            dma((2, 8, 2, 2)), dma((2, 8, 2, 2)),
            dma((8, 2, 2, 2)), dma((8, 2, 2, 2)),
            dma,
            dma((V, 2)), dma((V, 2)),
            dma((2, 8, 4)), dma((2, 8, 4)),
        ],
        compiler_params=pltpu.CompilerParams(
            collective_id=0, has_side_effects=True, vmem_limit_bytes=63 * 1024 * 1024
        ),
        name="rl_step",
    )(estimate, views, kernel_x, kernel_y, kernel_z, offsets)


def solution(mesh):
    in_specs = (P("depth", "tile", None), P(None, "depth", "tile", None), P(), P(), P(), P())
    return jax.shard_map(shards, mesh=mesh, in_specs=in_specs, out_specs=P("depth", "tile", None), check_vma=False)
```

```python
import jax
import jax.numpy as jnp
from jax import lax
from jax.experimental import pallas as pl
from jax.experimental.pallas import tpu as pltpu
from jax.sharding import PartitionSpec as P

MESH = pl.DeviceIdType.MESH
BF = jnp.bfloat16
F32 = jnp.float32
V = 8
T = 31
R = 32
H = 16
RH = R + 2 * H
NC = 1024
PAD = 128
CT = 256


def place(way, hop):
    if hop == 0:
        return 0, 0
    if hop == 8:
        return 0, 1
    return hop, way


GCOLS = ((0, 768), (768, 1024))
BTILES = ((0, 5), (5, 8))
STILES = ((0, 4), (4, 8))


def body(
    est_in, views, kx_in, ky_in, kz_in, offs_in, out,
    est, kx, ky, kz, offs, obuf, share,
    gath, acc, blur, corr, back, amat, bmat, xfwd, xbwd, yfwd, ybwd, vbuf, part, own, sbuf, rbuf,
    g_send, g_recv, h_send, h_recv, in_sem, o_sem, y_send, y_recv, r_send, r_recv,
):
    b = lax.axis_index("depth")
    t = lax.axis_index("tile")
    nz = lax.axis_size("depth")
    nt = lax.axis_size("tile")
    rows_total = R * nt
    view_rows = 5 * rows_total // 8
    zr = lax.rem(b + 1, nz)
    zl = lax.rem(b + nz - 1, nz)
    tu = lax.rem(t + nt - 1, nt)
    td = lax.rem(t + 1, nt)
    z_to = ((t, zr), (t, zl))
    t_to = ((tu, b), (td, b))

    loads = [
        pltpu.make_async_copy(src, dst, in_sem.at[i])
        for i, (src, dst) in enumerate(
            ((est_in, est), (kx_in, kx), (ky_in, ky), (kz_in, kz), (offs_in, offs), (views, vbuf))
        )
    ]
    for load in loads:
        load.start()
    barrier = pltpu.get_barrier_semaphore()
    corners = tuple((x, z) for x in (tu, td) for z in (zr, zl))
    for device in z_to + t_to + corners:
        pl.semaphore_signal(barrier, inc=1, device_id=device, device_id_type=MESH)

    def hop_copy(way, hop, q, k, c):
        pair, side = place(way, hop)
        pair2, side2 = place(way, hop + 1)
        rows = pl.ds(H + k * H, H) if c == 0 else pl.ds(H, R)
        cols = pl.ds(GCOLS[c][0], GCOLS[c][1] - GCOLS[c][0])
        sem = k if c == 0 else 2
        return pltpu.make_async_remote_copy(
            src_ref=gath.at[pair, side, q, rows, cols],
            dst_ref=gath.at[pair2, side2, q, rows, cols],
            send_sem=g_send.at[way, hop, q, sem],
            recv_sem=g_recv.at[way, hop, q, sem],
            device_id=z_to[way],
            device_id_type=MESH,
        )

    def halo_copy(pair, side, q, k, c):
        src, dst = ((H, H + R), (R, 0))[k]
        cols = pl.ds(GCOLS[c][0], GCOLS[c][1] - GCOLS[c][0])
        if (pair, side) == (0, 1):
            way = 1 - q
            pair2, side2 = place(way, 7)
            device = ((tu, td)[k], (zr, zl)[way])
            source = gath.at[pair2, side2, q, pl.ds(src, H), cols]
            target = gath.at[pair, side, q, pl.ds(dst, H), cols]
        else:
            device = t_to[k]
            source = gath.at[pair, side, :, pl.ds(src, H), cols]
            target = gath.at[pair, side, :, pl.ds(dst, H), cols]
        return pltpu.make_async_remote_copy(
            src_ref=source,
            dst_ref=target,
            send_sem=h_send.at[pair, side, q, k, c],
            recv_sem=h_recv.at[pair, side, q, k, c],
            device_id=device,
            device_id_type=MESH,
        )

    def halo_copies(pair, side, c):
        qs = (0, 1) if (pair, side) == (0, 1) else (0,)
        return [halo_copy(pair, side, q, k, c) for q in qs for k in range(2)]

    planes = ((1, 0), (0, 1))
    pieces = (((0, 0), (0, 1), (1, 0), (1, 1)), ((0, 0), (1, 0)))
    loads[0].wait()
    gath[0, 0, :, H : H + R, :] = est[...].astype(BF)
    pl.semaphore_wait(barrier, 8)
    for c in range(2):
        for i, k in pieces[c]:
            for way in range(2):
                hop_copy(way, 0, planes[way][i], k, c).start()
        for copy in halo_copies(0, 0, c):
            copy.start()
    for load in loads[1:5]:
        load.wait()

    lane = lax.broadcasted_iota(jnp.int32, (R, 2 * RH), 1)
    low = lane < RH
    src_row = jnp.where(low, lane, lane - RH)
    diff = src_row - lax.broadcasted_iota(jnp.int32, (R, 2 * RH), 0) - 1
    row_at = src_row + (t * R - H)
    exists = (row_at >= 0) & (row_at < rows_total)
    gap = lax.broadcasted_iota(jnp.int32, (PAD, PAD), 0) - lax.broadcasted_iota(jnp.int32, (PAD, PAD), 1)
    ring = jnp.where(gap + 15 < 0, gap + 15 + PAD, jnp.where(gap + 15 >= PAD, gap + 15 - PAD, gap + 15))

    def tables(v, carry):
        sx = kx[v, 0]
        sy = ky[v, 0]
        sz = kz[v, 0]
        for j in range(1, T):
            sx = sx + kx[v, j]
            sy = sy + ky[v, j]
            sz = sz + kz[v, j]
        xf = jnp.zeros((R, 2 * RH), F32)
        xb = jnp.zeros((R, 2 * RH), F32)
        cf = jnp.zeros((PAD, PAD), F32)
        cb = jnp.zeros((PAD, PAD), F32)
        for j in range(T):
            hit = diff == j
            xf = jnp.where(hit, kx[v, j], xf)
            xb = jnp.where(hit, kx[v, T - 1 - j], xb)
            hit = ring == j
            cf = jnp.where(hit, ky[v, j], cf)
            cb = jnp.where(hit, ky[v, T - 1 - j], cb)
        scale = jnp.full((R, 2 * RH), sx * sz, F32)
        xfwd[v] = jnp.where(exists, xf / scale, 0.0)
        xbwd[v] = jnp.where(exists, xb / scale, 0.0)
        for ref, c in ((yfwd, cf), (ybwd, cb)):
            c = c / jnp.full((PAD, PAD), sy, F32)
            bands = (
                jnp.where(gap >= PAD - 15, c, 0.0).astype(BF),
                jnp.where((gap <= 15) & (gap >= -15), c, 0.0).astype(BF),
                jnp.where(gap <= 15 - PAD, c, 0.0).astype(BF),
            )
            for i in range(3):
                ref[v, PAD * i : PAD * (i + 1), :] = bands[i]
        return carry

    lax.fori_loop(0, V, tables, 0)

    def mats(pair):
        offsets = (0, 8) if pair == 0 else (-pair, pair)
        zs = [2 * lax.rem(b + o + nz, nz) - 2 * b + 15 for o in offsets]

        def one(v, carry):
            xf = xfwd[v]
            xb = xbwd[v]
            c = {}
            for side in range(2):
                for q in range(2):
                    for p in range(2):
                        at = zs[side] + (q - p)
                        ok = (at >= 0) & (at < T)
                        c[side, q, p] = jnp.where(ok, kz[v, jnp.clip(at, 0, T - 1)], 0.0)
            for side in range(2):
                for p in range(2):
                    z = jnp.where(low, c[side, 0, p], c[side, 1, p])
                    amat[pair, pl.ds(pl.multiple_of(v * 64 + p * R, R), R), side * 128 : side * 128 + 128] = (xf * z).astype(BF)
                for q in range(2):
                    z = jnp.where(low, c[side, q, 0], c[side, q, 1])
                    first = side * 64 + q * R
                    bmat[pair, first : first + R, pl.ds(pl.multiple_of(v * 128, 128), 128)] = (xb * z).astype(BF)
            return carry

        lax.fori_loop(0, V, one, 0)

    def forward(pair, begin, end, chunk):
        def one(n, carry):
            cols = pl.ds(pl.multiple_of(n * CT, CT), CT)
            block = gath[pair, :, :, :, cols].reshape(4 * RH, CT)
            got = jnp.dot(amat[pair], block, preferred_element_type=F32)
            if not begin:
                got = got + acc[:, cols]
            if end:
                blur[:, pl.ds(pl.multiple_of(n * CT + PAD, PAD), CT)] = got.astype(BF)
            else:
                acc[:, cols] = got
            return carry

        lax.fori_loop(GCOLS[chunk][0] // CT, GCOLS[chunk][1] // CT, one, 0)

    for ref in (blur, corr):
        ref[:, :PAD] = jnp.zeros((ref.shape[0], PAD), BF)
        ref[:, PAD + NC :] = jnp.zeros((ref.shape[0], PAD), BF)
    rid = lax.broadcasted_iota(jnp.int32, (R, 128), 0) + t * R
    seen_by = jnp.zeros((R, 128), F32)
    for v in range(V):
        seen_by = seen_by + jnp.where((rid >= offs[v]) & (rid < offs[v] + view_rows), 1.0, 0.0)
    share[...] = 1.0 / jnp.maximum(seen_by, 1.0)

    def halos(pair, c):
        for side in range(2):
            for copy in halo_copies(pair, side, c):
                copy.wait_recv()

    for hop in range(1, 8):
        for c in range(2):
            for i, k in pieces[c]:
                for way in range(2):
                    q = planes[way][i]
                    hop_copy(way, hop - 1, q, k, c).wait_recv()
                    if hop < 7 or i == 0:
                        hop_copy(way, hop, q, k, c).start()
                    if hop == 7 and i == 0:
                        for kk in (k,) if c == 0 else (0, 1):
                            halo_copy(0, 1, q, kk, c).start()
            for side in range(2):
                for copy in halo_copies(hop, side, c):
                    copy.start()
        mats(hop)
        if hop >= 2:
            for c in range(2):
                halos(hop - 1, c)
                forward(hop - 1, hop == 2, False, c)
    mats(0)
    loads[5].wait()

    row = lax.broadcasted_iota(jnp.int32, (2 * R, 128), 0)
    row = jnp.where(row >= R, row - R, row) + t * R

    def y_copy(v, k, c):
        src, dst = ((H, H + R), (R, 0))[k]
        cols = pl.ds(STILES[c][0] * 128, (STILES[c][1] - STILES[c][0]) * 128)
        return pltpu.make_async_remote_copy(
            src_ref=back.at[v, :, pl.ds(src, H), cols],
            dst_ref=back.at[v, :, pl.ds(dst, H), cols],
            send_sem=y_send.at[v, k, c],
            recv_sem=y_recv.at[v, k, c],
            device_id=t_to[k],
            device_id_type=MESH,
        )

    def view_work(v, c):
        inside = (row >= offs[v]) & (row < offs[v] + view_rows)
        rows = pl.ds(pl.multiple_of(v * 64, 64), 64)
        tiles = range(*BTILES[c])
        lhs = jnp.concatenate([blur[rows, n * 128 : n * 128 + 384] for n in tiles], axis=0)
        blurred = jnp.dot(lhs, yfwd[v], preferred_element_type=F32)
        for i, n in enumerate(tiles):
            seen = vbuf[v, :, :, n * 128 : (n + 1) * 128].astype(F32).reshape(2 * R, 128)
            ratio = seen / blurred[i * 64 : (i + 1) * 64]
            corr[rows, PAD + n * 128 : PAD + (n + 1) * 128] = jnp.where(inside, ratio - 1.0, 0.0).astype(BF)
        tiles = range(*STILES[c])
        lhs = jnp.concatenate([corr[rows, n * 128 : n * 128 + 384] for n in tiles], axis=0)
        spread = jnp.dot(lhs, ybwd[v], preferred_element_type=F32).astype(BF)
        for i, n in enumerate(tiles):
            back[v, :, H : H + R, n * 128 : (n + 1) * 128] = spread[i * 64 : (i + 1) * 64].reshape(2, R, 128)

    def view_step(c):
        def step(i, carry):
            for v in (2 * i, 2 * i + 1):
                view_work(v, c)
            for v in (2 * i, 2 * i + 1):
                for k in range(2):
                    y_copy(v, k, c).start()
            return carry

        lax.fori_loop(0, V // 2, step, 0)

    for c in range(2):
        halos(7, c)
        forward(7, False, False, c)
        for i, k in pieces[c]:
            if i == 0:
                for way in range(2):
                    hop_copy(way, 7, planes[way][0], k, c).wait_recv()
        halos(0, c)
        forward(0, False, True, c)
        view_step(c)

    def y_wait(c):
        def one(v, carry):
            for k in range(2):
                y_copy(v, k, c).wait_recv()
            return carry

        return one

    def sum_copy(way, step, c, i):
        tiles = pl.ds(17 * c + 9 * i, 9 - i)
        return pltpu.make_async_remote_copy(
            src_ref=sbuf.at[way, step, tiles],
            dst_ref=rbuf.at[way, step, tiles],
            send_sem=r_send.at[way, step, c, i],
            recv_sem=r_recv.at[way, step, c, i],
            device_id=z_to[way],
            device_id_type=MESH,
        )

    def project(pair, target, c, first, last):
        def one(n, carry):
            cols = pl.ds(pl.multiple_of(n * CT, CT), CT)
            block = back[first:last, :, :, cols].reshape((last - first) * 2 * RH, CT)
            got = jnp.dot(bmat[pair, :, first * 128 : last * 128], block, preferred_element_type=F32)
            if first:
                got = got + target[:, cols]
            target[:, cols] = got
            return carry

        lax.fori_loop(STILES[c][0] // 2, STILES[c][1] // 2, one, 0)

    spots = tuple((k, j) for k in range(2) for j in range(4))
    orders = ((0, 1), (1, 0))

    def message(source, way, step, c, i):
        q = orders[way][i]
        at = (64 if step == 0 else (1 - way) * 64) + q * R
        tiles = [source[at + k * H : at + (k + 1) * H, 128 * (4 * c + j) : 128 * (4 * c + j + 1)] for k, j in spots]
        first = 17 * c + 1 + 8 * i
        if step > 1 or (step == 1 and i == 0):
            sum_copy(way, step - 1, c, i).wait_recv()
            base = rbuf[way, step - 1, 17 * c].astype(F32)
            tiles = [tiles[n] + (rbuf[way, step - 1, first + n].astype(F32) + base) for n in range(8)]
        if i == 0:
            mean = sum(tiles[1:], tiles[0]) * 0.125
            sbuf[way, step, 17 * c] = mean.astype(BF)
        mean = sbuf[way, step, 17 * c].astype(F32)
        for n in range(8):
            sbuf[way, step, first + n] = (tiles[n] - mean).astype(BF)
        sum_copy(way, step, c, i).start()

    early = 6
    for c in range(2):
        if c == 0:
            lax.fori_loop(0, V, y_wait(c), 0)
            project(0, own, c, 0, V)
        else:
            lax.fori_loop(0, early, y_wait(c), 0)
            project(0, own, c, 0, early)
            lax.fori_loop(early, V, y_wait(c), 0)
            project(0, own, c, early, V)
        for way in range(2):
            message(own, way, 0, c, 0)
        project(7, part, c, 0, V)
    for step in range(1, 8):
        for c in range(2):
            for i in range(2):
                for way in range(2):
                    message(part, way, step, c, i)
            if step < 7:
                project(7 - step, part, c, 0, V)

    def result(c, q):
        cols = pl.ds(STILES[c][0] * 128, (STILES[c][1] - STILES[c][0]) * 128)
        return pltpu.make_async_copy(obuf.at[q, :, cols], out.at[q, :, cols], o_sem.at[c, q])

    for c in range(2):
        for way in range(2):
            for i in range(2):
                sum_copy(way, 7, c, i).wait_recv()
        for q in range(2):
            bases = [rbuf[way, 7, 17 * c].astype(F32) for way in range(2)]
            for n, (k, j) in enumerate(spots):
                rows = slice(k * H, (k + 1) * H)
                cols = slice(128 * (4 * c + j), 128 * (4 * c + j + 1))
                total = own[q * R + k * H : q * R + (k + 1) * H, cols]
                for way in range(2):
                    total = total + (rbuf[way, 7, 17 * c + 1 + 8 * orders[way].index(q) + n].astype(F32) + bases[way])
                obuf[q, rows, cols] = est[q, rows, cols] * (1.0 + total * share[rows, :])
            result(c, q).start()

    for hop in range(8):
        for c in range(2):
            for way in range(2):
                for i, k in pieces[c]:
                    if hop < 7 or i == 0:
                        hop_copy(way, hop, planes[way][i], k, c).wait_send()
                for i in range(2):
                    if hop > 0 or i == 0:
                        sum_copy(way, hop, c, i).wait_send()
            for side in range(2):
                for copy in halo_copies(hop, side, c):
                    copy.wait_send()
    for c in range(2):
        for v in range(V):
            for k in range(2):
                y_copy(v, k, c).wait_send()
        for q in range(2):
            result(c, q).wait()


def shards(estimate, views, kernel_x, kernel_y, kernel_z, offsets):
    anywhere = pl.BlockSpec(memory_space=pl.ANY)
    dma = pltpu.SemaphoreType.DMA
    return pl.pallas_call(
        body,
        out_shape=jax.ShapeDtypeStruct(estimate.shape, F32),
        in_specs=[anywhere] * 6,
        out_specs=anywhere,
        scratch_shapes=[
            pltpu.VMEM((2, R, NC), F32),
            pltpu.SMEM(kernel_x.shape, F32),
            pltpu.SMEM(kernel_y.shape, F32),
            pltpu.SMEM(kernel_z.shape, F32),
            pltpu.SMEM(offsets.shape, jnp.int32),
            pltpu.VMEM((2, R, NC), F32),
            pltpu.VMEM((R, 128), F32),
            pltpu.VMEM((8, 2, 2, RH, NC), BF),
            pltpu.VMEM((V * 64, NC), F32),
            pltpu.VMEM((V * 64, NC + 2 * PAD), BF),
            pltpu.VMEM((V * 64, NC + 2 * PAD), BF),
            pltpu.VMEM((V, 2, RH, NC), BF),
            pltpu.VMEM((8, V * 64, 256), BF),
            pltpu.VMEM((8, 128, V * 128), BF),
            pltpu.VMEM((V, R, 128), F32),
            pltpu.VMEM((V, R, 128), F32),
            pltpu.VMEM((V, 384, 128), BF),
            pltpu.VMEM((V, 384, 128), BF),
            pltpu.VMEM((V, 2, R, NC), BF),
            pltpu.VMEM((128, NC), F32),
            pltpu.VMEM((128, NC), F32),
            pltpu.VMEM((2, 8, 34, H, 128), BF),
            pltpu.VMEM((2, 8, 34, H, 128), BF),
            dma((2, 8, 2, 3)), dma((2, 8, 2, 3)),
            dma((8, 2, 2, 2, 2)), dma((8, 2, 2, 2, 2)),
            dma((6,)), dma((2, 2)),
            dma((V, 2, 2)), dma((V, 2, 2)),
            dma((2, 8, 2, 2)), dma((2, 8, 2, 2)),
        ],
        compiler_params=pltpu.CompilerParams(
            collective_id=0, has_side_effects=True, vmem_limit_bytes=63 * 1024 * 1024
        ),
        name="rl_step",
    )(estimate, views, kernel_x, kernel_y, kernel_z, offsets)


def solution(mesh):
    in_specs = (P("depth", "tile", None), P(None, "depth", "tile", None), P(), P(), P(), P())
    return jax.shard_map(shards, mesh=mesh, in_specs=in_specs, out_specs=P("depth", "tile", None), check_vma=False)
```

```python
import jax
import jax.numpy as jnp
from jax import lax
from jax.experimental import pallas as pl
from jax.experimental.pallas import tpu as pltpu
from jax.sharding import PartitionSpec as P

MESH = pl.DeviceIdType.MESH
BF = jnp.bfloat16
F32 = jnp.float32
V = 8
T = 31
R = 32
H = 16
RH = R + 2 * H
NC = 1024
PAD = 128


def place(way, hop):
    if hop == 0:
        return 0, 0
    if hop == 8:
        return 0, 1
    return hop, way


GCOLS = ((0, 640), (640, 1024))
BTILES = ((0, 4), (4, 8))
STILES = ((0, 3), (3, 8))
SPOTS = tuple(tuple((k, n) for k in range(2) for n in range(*ends)) for ends in STILES)
FIRST = (0, 2 * len(SPOTS[0]) + 1)
LEAP = 4


def parent(leaps, d):
    return 0 if leaps and d == LEAP else d - 1


GLEAPS = (True, False)
SLEAPS = (False, True)


def body(
    est_in, views, kx_in, ky_in, kz_in, offs_in, out,
    est, kx, ky, kz, offs, obuf, share,
    gath, acc, blur, corr, back, amat, bmat, xfwd, xbwd, yfwd, ybwd, vbuf, part, own, sbuf, rbuf,
    g_send, g_recv, h_send, h_recv, in_sem, o_sem, y_send, y_recv, r_send, r_recv,
):
    b = lax.axis_index("depth")
    t = lax.axis_index("tile")
    nz = lax.axis_size("depth")
    nt = lax.axis_size("tile")
    rows_total = R * nt
    view_rows = 5 * rows_total // 8
    zr = lax.rem(b + 1, nz)
    zl = lax.rem(b + nz - 1, nz)
    tu = lax.rem(t + nt - 1, nt)
    td = lax.rem(t + 1, nt)
    z_to = ((t, zr), (t, zl))
    z_far = ((t, lax.rem(b + LEAP, nz)), (t, lax.rem(b + nz - LEAP, nz)))
    t_to = ((tu, b), (td, b))

    loads = [
        pltpu.make_async_copy(src, dst, in_sem.at[i])
        for i, (src, dst) in enumerate(
            ((est_in, est), (kx_in, kx), (ky_in, ky), (kz_in, kz), (offs_in, offs), (views, vbuf))
        )
    ]
    for load in loads:
        load.start()
    barrier = pltpu.get_barrier_semaphore()
    corners = tuple((x, z) for x in (tu, td) for z in (zr, zl))
    for device in z_to + z_far + t_to + corners:
        pl.semaphore_signal(barrier, inc=1, device_id=device, device_id_type=MESH)

    def hop_copy(way, d, q, k, c):
        source = parent(GLEAPS[c], d)
        pair, side = place(way, source)
        pair2, side2 = place(way, d)
        rows = pl.ds(H + k * H, H) if c == 0 else pl.ds(H, R)
        cols = pl.ds(GCOLS[c][0], GCOLS[c][1] - GCOLS[c][0])
        sem = k if c == 0 else 2
        return pltpu.make_async_remote_copy(
            src_ref=gath.at[pair, side, q, rows, cols],
            dst_ref=gath.at[pair2, side2, q, rows, cols],
            send_sem=g_send.at[way, d - 1, q, sem],
            recv_sem=g_recv.at[way, d - 1, q, sem],
            device_id=(z_to if d - source == 1 else z_far)[way],
            device_id_type=MESH,
        )

    def halo_copy(pair, side, q, k, c):
        src, dst = ((H, H + R), (R, 0))[k]
        cols = pl.ds(GCOLS[c][0], GCOLS[c][1] - GCOLS[c][0])
        if (pair, side) == (0, 1):
            way = 1 - q
            pair2, side2 = place(way, 7)
            device = ((tu, td)[k], (zr, zl)[way])
            source = gath.at[pair2, side2, q, pl.ds(src, H), cols]
            target = gath.at[pair, side, q, pl.ds(dst, H), cols]
        else:
            device = t_to[k]
            source = gath.at[pair, side, :, pl.ds(src, H), cols]
            target = gath.at[pair, side, :, pl.ds(dst, H), cols]
        return pltpu.make_async_remote_copy(
            src_ref=source,
            dst_ref=target,
            send_sem=h_send.at[pair, side, q, k, c],
            recv_sem=h_recv.at[pair, side, q, k, c],
            device_id=device,
            device_id_type=MESH,
        )

    def halo_copies(pair, side, c):
        qs = (0, 1) if (pair, side) == (0, 1) else (0,)
        return [halo_copy(pair, side, q, k, c) for q in qs for k in range(2)]

    planes = ((1, 0), (0, 1))
    pieces = (((0, 0), (0, 1), (1, 0), (1, 1)), ((0, 0), (1, 0)))
    loads[0].wait()
    gath[0, 0, :, H : H + R, :] = est[...].astype(BF)
    pl.semaphore_wait(barrier, 10)
    for c in range(2):
        for d in range(8, 0, -1):
            if parent(GLEAPS[c], d) == 0:
                for i, k in pieces[c]:
                    for way in range(2):
                        hop_copy(way, d, planes[way][i], k, c).start()
        for copy in halo_copies(0, 0, c):
            copy.start()
    for load in loads[1:5]:
        load.wait()

    lane = lax.broadcasted_iota(jnp.int32, (R, 2 * RH), 1)
    low = lane < RH
    src_row = jnp.where(low, lane, lane - RH)
    diff = src_row - lax.broadcasted_iota(jnp.int32, (R, 2 * RH), 0) - 1
    row_at = src_row + (t * R - H)
    exists = (row_at >= 0) & (row_at < rows_total)
    gap = lax.broadcasted_iota(jnp.int32, (PAD, PAD), 0) - lax.broadcasted_iota(jnp.int32, (PAD, PAD), 1)
    ring = jnp.where(gap + 15 < 0, gap + 15 + PAD, jnp.where(gap + 15 >= PAD, gap + 15 - PAD, gap + 15))

    def tables(v, carry):
        sx = kx[v, 0]
        sy = ky[v, 0]
        sz = kz[v, 0]
        for j in range(1, T):
            sx = sx + kx[v, j]
            sy = sy + ky[v, j]
            sz = sz + kz[v, j]
        xf = jnp.zeros((R, 2 * RH), F32)
        xb = jnp.zeros((R, 2 * RH), F32)
        cf = jnp.zeros((PAD, PAD), F32)
        cb = jnp.zeros((PAD, PAD), F32)
        for j in range(T):
            hit = diff == j
            xf = jnp.where(hit, kx[v, j], xf)
            xb = jnp.where(hit, kx[v, T - 1 - j], xb)
            hit = ring == j
            cf = jnp.where(hit, ky[v, j], cf)
            cb = jnp.where(hit, ky[v, T - 1 - j], cb)
        scale = jnp.full((R, 2 * RH), sx * sz, F32)
        xfwd[v] = jnp.where(exists, xf / scale, 0.0)
        xbwd[v] = jnp.where(exists, xb / scale, 0.0)
        for ref, c in ((yfwd, cf), (ybwd, cb)):
            c = c / jnp.full((PAD, PAD), sy, F32)
            bands = (
                jnp.where(gap >= PAD - 15, c, 0.0).astype(BF),
                jnp.where((gap <= 15) & (gap >= -15), c, 0.0).astype(BF),
                jnp.where(gap <= 15 - PAD, c, 0.0).astype(BF),
            )
            for i in range(3):
                ref[v, PAD * i : PAD * (i + 1), :] = bands[i]
        return carry

    lax.fori_loop(0, V, tables, 0)

    def mats(pair):
        offsets = (0, 8) if pair == 0 else (-pair, pair)
        zs = [2 * lax.rem(b + o + nz, nz) - 2 * b + 15 for o in offsets]

        def one(v, carry):
            xf = xfwd[v]
            xb = xbwd[v]
            c = {}
            for side in range(2):
                for q in range(2):
                    for p in range(2):
                        at = zs[side] + (q - p)
                        ok = (at >= 0) & (at < T)
                        c[side, q, p] = jnp.where(ok, kz[v, jnp.clip(at, 0, T - 1)], 0.0)
            for side in range(2):
                for p in range(2):
                    z = jnp.where(low, c[side, 0, p], c[side, 1, p])
                    amat[pair, pl.ds(pl.multiple_of(v * 64 + p * R, R), R), side * 128 : side * 128 + 128] = (xf * z).astype(BF)
                for q in range(2):
                    z = jnp.where(low, c[side, q, 0], c[side, q, 1])
                    first = side * 64 + q * R
                    bmat[pair, first : first + R, pl.ds(pl.multiple_of(v * 128, 128), 128)] = (xb * z).astype(BF)
            return carry

        lax.fori_loop(0, V, one, 0)

    def forward(pair, begin, end, chunk):
        def one(n, carry):
            cols = pl.ds(pl.multiple_of(n * 128, 128), 128)
            block = gath[pair, :, :, :, cols].reshape(4 * RH, 128)
            got = jnp.dot(amat[pair], block, preferred_element_type=F32)
            if not begin:
                got = got + acc[:, cols]
            if end:
                blur[:, pl.ds(pl.multiple_of(n * 128 + PAD, PAD), 128)] = got.astype(BF)
            else:
                acc[:, cols] = got
            return carry

        lax.fori_loop(GCOLS[chunk][0] // 128, GCOLS[chunk][1] // 128, one, 0)

    for ref in (blur, corr):
        ref[:, :PAD] = jnp.zeros((ref.shape[0], PAD), BF)
        ref[:, PAD + NC :] = jnp.zeros((ref.shape[0], PAD), BF)
    rid = lax.broadcasted_iota(jnp.int32, (R, 128), 0) + t * R
    seen_by = jnp.zeros((R, 128), F32)
    for v in range(V):
        seen_by = seen_by + jnp.where((rid >= offs[v]) & (rid < offs[v] + view_rows), 1.0, 0.0)
    share[...] = 1.0 / jnp.maximum(seen_by, 1.0)

    def halos(pair, c):
        for side in range(2):
            for copy in halo_copies(pair, side, c):
                copy.wait_recv()

    def arrive(c, d):
        for i, k in pieces[c]:
            for way in range(2):
                q = planes[way][i]
                if d < 8 or i == 0:
                    hop_copy(way, d, q, k, c).wait_recv()
                if d < 7 and parent(GLEAPS[c], d + 1) == d or d == 7 and i == 0:
                    hop_copy(way, d + 1, q, k, c).start()
                if d == 7 and i == 0:
                    for kk in (k,) if c == 0 else (0, 1):
                        halo_copy(0, 1, q, kk, c).start()
        if d < 8:
            for side in range(2):
                for copy in halo_copies(d, side, c):
                    copy.start()

    ready = set()
    waiting = []

    def combine(c, d):
        pair = d % 8
        if pair not in ready:
            ready.add(pair)
            mats(pair)
        halos(pair, c)
        forward(pair, d == 1, d == 8, c)

    def gather(c, d):
        arrive(c, d)
        waiting.append((c, d))
        if len(waiting) > 2:
            combine(*waiting.pop(0))

    row = lax.broadcasted_iota(jnp.int32, (2 * R, 128), 0)
    row = jnp.where(row >= R, row - R, row) + t * R

    def y_copy(v, k, c):
        src, dst = ((H, H + R), (R, 0))[k]
        cols = pl.ds(STILES[c][0] * 128, (STILES[c][1] - STILES[c][0]) * 128)
        return pltpu.make_async_remote_copy(
            src_ref=back.at[v, :, pl.ds(src, H), cols],
            dst_ref=back.at[v, :, pl.ds(dst, H), cols],
            send_sem=y_send.at[v, k, c],
            recv_sem=y_recv.at[v, k, c],
            device_id=t_to[k],
            device_id_type=MESH,
        )

    def view_work(v, c):
        inside = (row >= offs[v]) & (row < offs[v] + view_rows)
        rows = pl.ds(pl.multiple_of(v * 64, 64), 64)
        tiles = range(*BTILES[c])
        lhs = jnp.concatenate([blur[rows, n * 128 : n * 128 + 384] for n in tiles], axis=0)
        blurred = jnp.dot(lhs, yfwd[v], preferred_element_type=F32)
        for i, n in enumerate(tiles):
            seen = vbuf[v, :, :, n * 128 : (n + 1) * 128].astype(F32).reshape(2 * R, 128)
            ratio = seen / blurred[i * 64 : (i + 1) * 64]
            corr[rows, PAD + n * 128 : PAD + (n + 1) * 128] = jnp.where(inside, ratio - 1.0, 0.0).astype(BF)
        tiles = range(*STILES[c])
        lhs = jnp.concatenate([corr[rows, n * 128 : n * 128 + 384] for n in tiles], axis=0)
        spread = jnp.dot(lhs, ybwd[v], preferred_element_type=F32).astype(BF)
        for i, n in enumerate(tiles):
            back[v, :, H : H + R, n * 128 : (n + 1) * 128] = spread[i * 64 : (i + 1) * 64].reshape(2, R, 128)

    def view_step(c, first, last):
        def step(i, carry):
            for v in (2 * i, 2 * i + 1):
                view_work(v, c)
            for v in (2 * i, 2 * i + 1):
                for k in range(2):
                    y_copy(v, k, c).start()
            return carry

        lax.fori_loop(first // 2, last // 2, step, 0)

    def y_wait(c):
        def one(v, carry):
            for k in range(2):
                y_copy(v, k, c).wait_recv()
            return carry

        return one

    def sum_copy(way, d, c, i):
        count = len(SPOTS[c])
        tiles = pl.ds(FIRST[c] + (count + 1) * i, count + 1 - i)
        return pltpu.make_async_remote_copy(
            src_ref=sbuf.at[way, d - 1, tiles],
            dst_ref=rbuf.at[way, d - 1, tiles],
            send_sem=r_send.at[way, d - 1, c, i],
            recv_sem=r_recv.at[way, d - 1, c, i],
            device_id=(z_to if d - parent(SLEAPS[c], d) == 1 else z_far)[way],
            device_id_type=MESH,
        )

    def project(pair, target, c, first, last):
        def one(n, carry):
            cols = pl.ds(pl.multiple_of(n * 128, 128), 128)
            block = back[first:last, :, :, cols].reshape((last - first) * 2 * RH, 128)
            got = jnp.dot(bmat[pair, :, first * 128 : last * 128], block, preferred_element_type=F32)
            if first:
                got = got + target[:, cols]
            target[:, cols] = got
            return carry

        lax.fori_loop(STILES[c][0], STILES[c][1], one, 0)

    orders = ((0, 1), (1, 0))

    def message(way, d, c, i):
        q = orders[way][i]
        source = own if d == 8 else part
        at = (64 if d == 8 else (1 - way) * 64) + q * R
        count = len(SPOTS[c])
        tiles = [source[at + k * H : at + (k + 1) * H, 128 * n : 128 * (n + 1)] for k, n in SPOTS[c]]
        first = FIRST[c] + 1 + count * i
        if d < 8 and parent(SLEAPS[c], d + 1) == d and (d < 7 or i == 0):
            sum_copy(way, d + 1, c, i).wait_recv()
            base = rbuf[way, d, FIRST[c]].astype(F32)
            tiles = [tiles[n] + (rbuf[way, d, first + n].astype(F32) + base) for n in range(count)]
        if i == 0:
            mean = sum(tiles[1:], tiles[0]) * (1.0 / count)
            sbuf[way, d - 1, FIRST[c]] = mean.astype(BF)
        mean = sbuf[way, d - 1, FIRST[c]].astype(F32)
        for n in range(count):
            sbuf[way, d - 1, first + n] = (tiles[n] - mean).astype(BF)
        sum_copy(way, d, c, i).start()

    sequence = ((8, 7, 6, 5, 4, 3, 2, 1), (8, 3, 7, 2, 6, 1, 5, 4))

    def send_sums(c, d):
        for i in range(2 if d < 8 else 1):
            for way in range(2):
                message(way, d, c, i)
        if d != sequence[c][-1]:
            project(sequence[c][sequence[c].index(d) + 1], part, c, 0, V)

    def result(c, q):
        cols = pl.ds(STILES[c][0] * 128, (STILES[c][1] - STILES[c][0]) * 128)
        return pltpu.make_async_copy(obuf.at[q, :, cols], out.at[q, :, cols], o_sem.at[c, q])

    def finish(c):
        count = len(SPOTS[c])
        last = [d for d in range(1, 9) if parent(SLEAPS[c], d) == 0]
        for d in last:
            for way in range(2):
                for i in range(2):
                    sum_copy(way, d, c, i).wait_recv()
        for q in range(2):
            base = sum(rbuf[way, d - 1, FIRST[c]].astype(F32) for way in range(2) for d in last)
            for m, (k, n) in enumerate(SPOTS[c]):
                rows = slice(k * H, (k + 1) * H)
                cols = slice(128 * n, 128 * (n + 1))
                total = own[q * R + k * H : q * R + (k + 1) * H, cols] + base
                for way in range(2):
                    for d in last:
                        total = total + rbuf[way, d - 1, FIRST[c] + 1 + count * orders[way].index(q) + m].astype(F32)
                obuf[q, rows, cols] = est[q, rows, cols] * (1.0 + total * share[rows, :])
            result(c, q).start()

    for c, d in ((0, 1), (1, 1), (0, 4), (0, 2), (1, 2), (0, 5), (0, 3), (1, 3), (0, 6), (1, 4), (0, 7), (1, 5)):
        gather(c, d)
    while any(c == 0 for c, d in waiting):
        combine(*waiting.pop(0))
    loads[5].wait()
    arrive(0, 8)
    combine(0, 8)
    view_step(0, 0, 4)
    gather(1, 6)
    view_step(0, 4, 8)
    gather(1, 7)
    while waiting:
        combine(*waiting.pop(0))
    lax.fori_loop(0, V, y_wait(0), 0)
    project(0, own, 0, 0, V)
    send_sums(0, 8)
    arrive(1, 8)
    combine(1, 8)
    view_step(1, 0, 8)
    send_sums(0, 7)
    early = 6
    lax.fori_loop(0, early, y_wait(1), 0)
    project(0, own, 1, 0, early)
    lax.fori_loop(early, V, y_wait(1), 0)
    project(0, own, 1, early, V)
    for c, d in (
        (1, 8), (1, 3), (0, 6), (1, 7), (1, 2), (0, 5), (1, 6), (1, 1), (0, 4), (1, 5), (0, 3), (1, 4), (0, 2), (0, 1),
    ):
        send_sums(c, d)
    for c in range(2):
        finish(c)

    for d in range(1, 9):
        for c in range(2):
            for way in range(2):
                for i, k in pieces[c]:
                    if d < 8 or i == 0:
                        hop_copy(way, d, planes[way][i], k, c).wait_send()
                for i in range(2 if d < 8 else 1):
                    sum_copy(way, d, c, i).wait_send()
            for side in range(2):
                for copy in halo_copies(d % 8, side, c):
                    copy.wait_send()
    for c in range(2):
        for v in range(V):
            for k in range(2):
                y_copy(v, k, c).wait_send()
        for q in range(2):
            result(c, q).wait()


def shards(estimate, views, kernel_x, kernel_y, kernel_z, offsets):
    anywhere = pl.BlockSpec(memory_space=pl.ANY)
    dma = pltpu.SemaphoreType.DMA
    return pl.pallas_call(
        body,
        out_shape=jax.ShapeDtypeStruct(estimate.shape, F32),
        in_specs=[anywhere] * 6,
        out_specs=anywhere,
        scratch_shapes=[
            pltpu.VMEM((2, R, NC), F32),
            pltpu.SMEM(kernel_x.shape, F32),
            pltpu.SMEM(kernel_y.shape, F32),
            pltpu.SMEM(kernel_z.shape, F32),
            pltpu.SMEM(offsets.shape, jnp.int32),
            pltpu.VMEM((2, R, NC), F32),
            pltpu.VMEM((R, 128), F32),
            pltpu.VMEM((8, 2, 2, RH, NC), BF),
            pltpu.VMEM((V * 64, NC), F32),
            pltpu.VMEM((V * 64, NC + 2 * PAD), BF),
            pltpu.VMEM((V * 64, NC + 2 * PAD), BF),
            pltpu.VMEM((V, 2, RH, NC), BF),
            pltpu.VMEM((8, V * 64, 256), BF),
            pltpu.VMEM((8, 128, V * 128), BF),
            pltpu.VMEM((V, R, 128), F32),
            pltpu.VMEM((V, R, 128), F32),
            pltpu.VMEM((V, 384, 128), BF),
            pltpu.VMEM((V, 384, 128), BF),
            pltpu.VMEM((V, 2, R, NC), BF),
            pltpu.VMEM((128, NC), F32),
            pltpu.VMEM((128, NC), F32),
            pltpu.VMEM((2, 8, 34, H, 128), BF),
            pltpu.VMEM((2, 8, 34, H, 128), BF),
            dma((2, 8, 2, 3)), dma((2, 8, 2, 3)),
            dma((8, 2, 2, 2, 2)), dma((8, 2, 2, 2, 2)),
            dma((6,)), dma((2, 2)),
            dma((V, 2, 2)), dma((V, 2, 2)),
            dma((2, 8, 2, 2)), dma((2, 8, 2, 2)),
        ],
        compiler_params=pltpu.CompilerParams(
            collective_id=0, has_side_effects=True, vmem_limit_bytes=63 * 1024 * 1024
        ),
        name="rl_step",
    )(estimate, views, kernel_x, kernel_y, kernel_z, offsets)


def solution(mesh):
    in_specs = (P("depth", "tile", None), P(None, "depth", "tile", None), P(), P(), P(), P())
    return jax.shard_map(shards, mesh=mesh, in_specs=in_specs, out_specs=P("depth", "tile", None), check_vma=False)
```

```python
import jax
import jax.numpy as jnp
from jax import lax
from jax.experimental import pallas as pl
from jax.experimental.pallas import tpu as pltpu
from jax.sharding import PartitionSpec as P

MESH = pl.DeviceIdType.MESH
BF = jnp.bfloat16
F32 = jnp.float32
V = 8
T = 31
R = 32
H = 16
RH = R + 2 * H
NC = 1024
PAD = 128
CT = 256


def place(way, hop):
    if hop == 0:
        return 0, 0
    if hop == 8:
        return 0, 1
    return hop, way


GCOLS = ((0, 768), (768, 1024))
BTILES = ((0, 5), (5, 8))
STILES = ((0, 4), (4, 8))

SINGLY = ((0, 1), (7, 0), (7, 1))
DIAGONAL = ((0, 1),)


def body(
    est_in, views, kx_in, ky_in, kz_in, offs_in, out,
    est, kx, ky, kz, offs, obuf, share,
    gath, acc, blur, corr, back, amat, bmat, xfwd, xbwd, yfwd, ybwd, vbuf, part, own, sbuf, rbuf,
    g_send, g_recv, h_send, h_recv, in_sem, o_sem, y_send, y_recv, r_send, r_recv,
):
    b = lax.axis_index("depth")
    t = lax.axis_index("tile")
    nz = lax.axis_size("depth")
    nt = lax.axis_size("tile")
    rows_total = R * nt
    view_rows = 5 * rows_total // 8
    zr = lax.rem(b + 1, nz)
    zl = lax.rem(b + nz - 1, nz)
    tu = lax.rem(t + nt - 1, nt)
    td = lax.rem(t + 1, nt)
    z_to = ((t, zr), (t, zl))
    t_to = ((tu, b), (td, b))

    loads = [
        pltpu.make_async_copy(src, dst, in_sem.at[i])
        for i, (src, dst) in enumerate(
            ((est_in, est), (kx_in, kx), (ky_in, ky), (kz_in, kz), (offs_in, offs), (views, vbuf))
        )
    ]
    for load in loads:
        load.start()
    barrier = pltpu.get_barrier_semaphore()
    corners = tuple((x, z) for x in (tu, td) for z in (zr, zl))
    for device in z_to + t_to + corners:
        pl.semaphore_signal(barrier, inc=1, device_id=device, device_id_type=MESH)

    def hop_copy(way, hop, q, k, c):
        pair, side = place(way, hop)
        pair2, side2 = place(way, hop + 1)
        rows = pl.ds(H + k * H, H) if c == 0 else pl.ds(H, R)
        cols = pl.ds(GCOLS[c][0], GCOLS[c][1] - GCOLS[c][0])
        sem = k if c == 0 else 2
        return pltpu.make_async_remote_copy(
            src_ref=gath.at[pair, side, q, rows, cols],
            dst_ref=gath.at[pair2, side2, q, rows, cols],
            send_sem=g_send.at[way, hop, q, sem],
            recv_sem=g_recv.at[way, hop, q, sem],
            device_id=z_to[way],
            device_id_type=MESH,
        )

    def halo_copy(pair, side, q, k, c):
        src, dst = ((H, H + R), (R, 0))[k]
        cols = pl.ds(GCOLS[c][0], GCOLS[c][1] - GCOLS[c][0])
        if (pair, side) in SINGLY:
            pair2, side2, device = pair, side, t_to[k]
            if (pair, side) in DIAGONAL:
                way = side if pair else 1 - q
                pair2, side2 = place(way, (pair or 8) - 1)
                device = ((tu, td)[k], (zr, zl)[way])
            source = gath.at[pair2, side2, q, pl.ds(src, H), cols]
            target = gath.at[pair, side, q, pl.ds(dst, H), cols]
        else:
            device = t_to[k]
            source = gath.at[pair, side, :, pl.ds(src, H), cols]
            target = gath.at[pair, side, :, pl.ds(dst, H), cols]
        return pltpu.make_async_remote_copy(
            src_ref=source,
            dst_ref=target,
            send_sem=h_send.at[pair, side, q, k, c],
            recv_sem=h_recv.at[pair, side, q, k, c],
            device_id=device,
            device_id_type=MESH,
        )

    def halo_copies(pair, side, c):
        qs = (0, 1) if (pair, side) in SINGLY else (0,)
        return [halo_copy(pair, side, q, k, c) for q in qs for k in range(2)]

    planes = ((1, 0), (0, 1))
    pieces = (((0, 0), (0, 1), (1, 0), (1, 1)), ((0, 0), (1, 0)))
    loads[0].wait()
    gath[0, 0, :, H : H + R, :] = est[...].astype(BF)
    pl.semaphore_wait(barrier, 8)
    for c in range(2):
        for i, k in pieces[c]:
            for way in range(2):
                hop_copy(way, 0, planes[way][i], k, c).start()
        for copy in halo_copies(0, 0, c):
            copy.start()
    for load in loads[1:5]:
        load.wait()

    lane = lax.broadcasted_iota(jnp.int32, (R, 2 * RH), 1)
    low = lane < RH
    src_row = jnp.where(low, lane, lane - RH)
    diff = src_row - lax.broadcasted_iota(jnp.int32, (R, 2 * RH), 0) - 1
    row_at = src_row + (t * R - H)
    exists = (row_at >= 0) & (row_at < rows_total)
    gap = lax.broadcasted_iota(jnp.int32, (PAD, PAD), 0) - lax.broadcasted_iota(jnp.int32, (PAD, PAD), 1)
    ring = jnp.where(gap + 15 < 0, gap + 15 + PAD, jnp.where(gap + 15 >= PAD, gap + 15 - PAD, gap + 15))

    def tables(v, carry):
        sx = kx[v, 0]
        sy = ky[v, 0]
        sz = kz[v, 0]
        for j in range(1, T):
            sx = sx + kx[v, j]
            sy = sy + ky[v, j]
            sz = sz + kz[v, j]
        xf = jnp.zeros((R, 2 * RH), F32)
        xb = jnp.zeros((R, 2 * RH), F32)
        cf = jnp.zeros((PAD, PAD), F32)
        cb = jnp.zeros((PAD, PAD), F32)
        for j in range(T):
            hit = diff == j
            xf = jnp.where(hit, kx[v, j], xf)
            xb = jnp.where(hit, kx[v, T - 1 - j], xb)
            hit = ring == j
            cf = jnp.where(hit, ky[v, j], cf)
            cb = jnp.where(hit, ky[v, T - 1 - j], cb)
        scale = jnp.full((R, 2 * RH), sx * sz, F32)
        xfwd[v] = jnp.where(exists, xf / scale, 0.0)
        xbwd[v] = jnp.where(exists, xb / scale, 0.0)
        for ref, c in ((yfwd, cf), (ybwd, cb)):
            c = c / jnp.full((PAD, PAD), sy, F32)
            bands = (
                jnp.where(gap >= PAD - 15, c, 0.0).astype(BF),
                jnp.where((gap <= 15) & (gap >= -15), c, 0.0).astype(BF),
                jnp.where(gap <= 15 - PAD, c, 0.0).astype(BF),
            )
            for i in range(3):
                ref[v, PAD * i : PAD * (i + 1), :] = bands[i]
        return carry

    lax.fori_loop(0, V, tables, 0)

    def mats(pair):
        offsets = (0, 8) if pair == 0 else (-pair, pair)
        zs = [2 * lax.rem(b + o + nz, nz) - 2 * b + 15 for o in offsets]

        def one(v, carry):
            xf = xfwd[v]
            xb = xbwd[v]
            c = {}
            for side in range(2):
                for q in range(2):
                    for p in range(2):
                        at = zs[side] + (q - p)
                        ok = (at >= 0) & (at < T)
                        c[side, q, p] = jnp.where(ok, kz[v, jnp.clip(at, 0, T - 1)], 0.0)
            for side in range(2):
                for p in range(2):
                    z = jnp.where(low, c[side, 0, p], c[side, 1, p])
                    amat[pair, pl.ds(pl.multiple_of(v * 64 + p * R, R), R), side * 128 : side * 128 + 128] = (xf * z).astype(BF)
                for q in range(2):
                    z = jnp.where(low, c[side, q, 0], c[side, q, 1])
                    first = side * 64 + q * R
                    bmat[pair, first : first + R, pl.ds(pl.multiple_of(v * 128, 128), 128)] = (xb * z).astype(BF)
            return carry

        lax.fori_loop(0, V, one, 0)

    def forward(pair, begin, end, chunk):
        def one(n, carry):
            cols = pl.ds(pl.multiple_of(n * CT, CT), CT)
            block = gath[pair, :, :, :, cols].reshape(4 * RH, CT)
            got = jnp.dot(amat[pair], block, preferred_element_type=F32)
            if not begin:
                got = got + acc[:, cols]
            if end:
                blur[:, pl.ds(pl.multiple_of(n * CT + PAD, PAD), CT)] = got.astype(BF)
            else:
                acc[:, cols] = got
            return carry

        lax.fori_loop(GCOLS[chunk][0] // CT, GCOLS[chunk][1] // CT, one, 0)

    blur[:, :PAD] = jnp.zeros((V * 64, PAD), BF)
    blur[:, PAD + NC :] = jnp.zeros((V * 64, PAD), BF)
    rid = lax.broadcasted_iota(jnp.int32, (R, 128), 0) + t * R
    seen_by = jnp.zeros((R, 128), F32)
    for v in range(V):
        seen_by = seen_by + jnp.where((rid >= offs[v]) & (rid < offs[v] + view_rows), 1.0, 0.0)
    share[...] = 1.0 / jnp.maximum(seen_by, 1.0)

    def halos(pair, c):
        for side in range(2):
            for copy in halo_copies(pair, side, c):
                copy.wait_recv()

    for hop in range(1, 8):
        for c in range(2):
            for i, k in pieces[c]:
                for way in range(2):
                    q = planes[way][i]
                    hop_copy(way, hop - 1, q, k, c).wait_recv()
                    if hop < 7 or i == 0:
                        hop_copy(way, hop, q, k, c).start()
                    for kk in (k,) if c == 0 else (0, 1):
                        if hop == 7 and i == 0:
                            halo_copy(0, 1, q, kk, c).start()
                        if hop == 7:
                            halo_copy(7, way, q, kk, c).start()
            if hop < 7:
                for side in range(2):
                    for copy in halo_copies(hop, side, c):
                        copy.start()
        mats(hop)
        if hop >= 2:
            for c in range(2):
                halos(hop - 1, c)
                forward(hop - 1, hop == 2, False, c)
    mats(0)
    loads[5].wait()

    row = lax.broadcasted_iota(jnp.int32, (2 * R, 128), 0)
    row = jnp.where(row >= R, row - R, row) + t * R

    def y_copy(v, k, c):
        src, dst = ((H, H + R), (R, 0))[k]
        cols = pl.ds(STILES[c][0] * 128, (STILES[c][1] - STILES[c][0]) * 128)
        return pltpu.make_async_remote_copy(
            src_ref=back.at[v, :, pl.ds(src, H), cols],
            dst_ref=back.at[v, :, pl.ds(dst, H), cols],
            send_sem=y_send.at[v, k, c],
            recv_sem=y_recv.at[v, k, c],
            device_id=t_to[k],
            device_id_type=MESH,
        )

    def view_work(v, c):
        inside = (row >= offs[v]) & (row < offs[v] + view_rows)
        rows = pl.ds(pl.multiple_of(v * 64, 64), 64)
        tiles = range(*BTILES[c])
        lhs = jnp.concatenate([blur[rows, n * 128 : n * 128 + 384] for n in tiles], axis=0)
        blurred = jnp.dot(lhs, yfwd[v], preferred_element_type=F32)
        none = jnp.zeros((2 * R, 128), BF)
        fixes = {-1: none, NC // 128: none}
        if c == 1:
            fixes[tiles[0] - 2] = corr[rows, :128]
            fixes[tiles[0] - 1] = corr[rows, 128:]
        for i, n in enumerate(tiles):
            seen = vbuf[v, :, :, n * 128 : (n + 1) * 128].astype(F32).reshape(2 * R, 128)
            ratio = seen / blurred[i * 64 : (i + 1) * 64]
            fixes[n] = jnp.where(inside, ratio - 1.0, 0.0).astype(BF)
        if c == 0:
            corr[rows, :128] = fixes[tiles[-1] - 1]
            corr[rows, 128:] = fixes[tiles[-1]]
        tiles = range(*STILES[c])
        lhs = jnp.concatenate([jnp.concatenate([fixes[n - 1], fixes[n], fixes[n + 1]], axis=1) for n in tiles], axis=0)
        spread = jnp.dot(lhs, ybwd[v], preferred_element_type=F32).astype(BF)
        for i, n in enumerate(tiles):
            back[v, :, H : H + R, n * 128 : (n + 1) * 128] = spread[i * 64 : (i + 1) * 64].reshape(2, R, 128)

    def view_step(c):
        def step(i, carry):
            for v in (2 * i, 2 * i + 1):
                view_work(v, c)
            for v in (2 * i, 2 * i + 1):
                for k in range(2):
                    y_copy(v, k, c).start()
            return carry

        lax.fori_loop(0, V // 2, step, 0)

    for c in range(2):
        halos(7, c)
        forward(7, False, False, c)
        for i, k in pieces[c]:
            if i == 0:
                for way in range(2):
                    hop_copy(way, 7, planes[way][0], k, c).wait_recv()
        halos(0, c)
        forward(0, False, True, c)
        view_step(c)

    def y_wait(c):
        def one(v, carry):
            for k in range(2):
                y_copy(v, k, c).wait_recv()
            return carry

        return one

    def sum_copy(way, step, c, i):
        tiles = pl.ds(17 * c + 9 * i, 9 - i)
        return pltpu.make_async_remote_copy(
            src_ref=sbuf.at[way, step, tiles],
            dst_ref=rbuf.at[way, step, tiles],
            send_sem=r_send.at[way, step, c, i],
            recv_sem=r_recv.at[way, step, c, i],
            device_id=z_to[way],
            device_id_type=MESH,
        )

    def project(pair, target, c, first, last):
        def one(n, carry):
            cols = pl.ds(pl.multiple_of(n * CT, CT), CT)
            block = back[first:last, :, :, cols].reshape((last - first) * 2 * RH, CT)
            got = jnp.dot(bmat[pair, :, first * 128 : last * 128], block, preferred_element_type=F32)
            if first:
                got = got + target[:, cols]
            target[:, cols] = got
            return carry

        lax.fori_loop(STILES[c][0] // 2, STILES[c][1] // 2, one, 0)

    spots = tuple((k, j) for k in range(2) for j in range(4))
    orders = ((0, 1), (1, 0))

    def message(source, way, step, c, i):
        q = orders[way][i]
        at = (64 if step == 0 else (1 - way) * 64) + q * R
        tiles = [source[at + k * H : at + (k + 1) * H, 128 * (4 * c + j) : 128 * (4 * c + j + 1)] for k, j in spots]
        first = 17 * c + 1 + 8 * i
        if step > 1 or (step == 1 and i == 0):
            sum_copy(way, step - 1, c, i).wait_recv()
            base = rbuf[way, step - 1, 17 * c].astype(F32)
            tiles = [tiles[n] + (rbuf[way, step - 1, first + n].astype(F32) + base) for n in range(8)]
        if i == 0:
            mean = sum(tiles[1:], tiles[0]) * 0.125
            sbuf[way, step, 17 * c] = mean.astype(BF)
        mean = sbuf[way, step, 17 * c].astype(F32)
        for n in range(8):
            sbuf[way, step, first + n] = (tiles[n] - mean).astype(BF)
        sum_copy(way, step, c, i).start()

    early = 6
    for c in range(2):
        if c == 0:
            lax.fori_loop(0, V, y_wait(c), 0)
            project(0, own, c, 0, V)
        else:
            lax.fori_loop(0, early, y_wait(c), 0)
            project(0, own, c, 0, early)
            lax.fori_loop(early, V, y_wait(c), 0)
            project(0, own, c, early, V)
        for way in range(2):
            message(own, way, 0, c, 0)
        project(7, part, c, 0, V)
    for step in range(1, 8):
        for c in range(2):
            for i in range(2):
                for way in range(2):
                    message(part, way, step, c, i)
            if step < 7:
                project(7 - step, part, c, 0, V)

    def result(c, q):
        cols = pl.ds(STILES[c][0] * 128, (STILES[c][1] - STILES[c][0]) * 128)
        return pltpu.make_async_copy(obuf.at[q, :, cols], out.at[q, :, cols], o_sem.at[c, q])

    for c in range(2):
        for way in range(2):
            for i in range(2):
                sum_copy(way, 7, c, i).wait_recv()
        for q in range(2):
            bases = [rbuf[way, 7, 17 * c].astype(F32) for way in range(2)]
            for n, (k, j) in enumerate(spots):
                rows = slice(k * H, (k + 1) * H)
                cols = slice(128 * (4 * c + j), 128 * (4 * c + j + 1))
                total = own[q * R + k * H : q * R + (k + 1) * H, cols]
                for way in range(2):
                    total = total + (rbuf[way, 7, 17 * c + 1 + 8 * orders[way].index(q) + n].astype(F32) + bases[way])
                obuf[q, rows, cols] = total * share[rows, :]
            result(c, q).start()

    for hop in range(8):
        for c in range(2):
            for way in range(2):
                for i, k in pieces[c]:
                    if hop < 7 or i == 0:
                        hop_copy(way, hop, planes[way][i], k, c).wait_send()
                for i in range(2):
                    if hop > 0 or i == 0:
                        sum_copy(way, hop, c, i).wait_send()
            for side in range(2):
                for copy in halo_copies(hop, side, c):
                    copy.wait_send()
    for c in range(2):
        for v in range(V):
            for k in range(2):
                y_copy(v, k, c).wait_send()
        for q in range(2):
            result(c, q).wait()


def shards(estimate, views, kernel_x, kernel_y, kernel_z, offsets):
    anywhere = pl.BlockSpec(memory_space=pl.ANY)
    dma = pltpu.SemaphoreType.DMA
    change = pl.pallas_call(
        body,
        out_shape=jax.ShapeDtypeStruct(estimate.shape, F32),
        in_specs=[anywhere] * 6,
        out_specs=anywhere,
        scratch_shapes=[
            pltpu.VMEM((2, R, NC), F32),
            pltpu.SMEM(kernel_x.shape, F32),
            pltpu.SMEM(kernel_y.shape, F32),
            pltpu.SMEM(kernel_z.shape, F32),
            pltpu.SMEM(offsets.shape, jnp.int32),
            pltpu.VMEM((2, R, NC), F32),
            pltpu.VMEM((R, 128), F32),
            pltpu.VMEM((8, 2, 2, RH, NC), BF),
            pltpu.VMEM((V * 64, NC), F32),
            pltpu.VMEM((V * 64, NC + 2 * PAD), BF),
            pltpu.VMEM((V * 64, 256), BF),
            pltpu.VMEM((V, 2, RH, NC), BF),
            pltpu.VMEM((8, V * 64, 256), BF),
            pltpu.VMEM((8, 128, V * 128), BF),
            pltpu.VMEM((V, R, 128), F32),
            pltpu.VMEM((V, R, 128), F32),
            pltpu.VMEM((V, 384, 128), BF),
            pltpu.VMEM((V, 384, 128), BF),
            pltpu.VMEM((V, 2, R, NC), BF),
            pltpu.VMEM((128, NC), F32),
            pltpu.VMEM((128, NC), F32),
            pltpu.VMEM((2, 8, 34, H, 128), BF),
            pltpu.VMEM((2, 8, 34, H, 128), BF),
            dma((2, 8, 2, 3)), dma((2, 8, 2, 3)),
            dma((8, 2, 2, 2, 2)), dma((8, 2, 2, 2, 2)),
            dma((6,)), dma((2, 2)),
            dma((V, 2, 2)), dma((V, 2, 2)),
            dma((2, 8, 2, 2)), dma((2, 8, 2, 2)),
        ],
        compiler_params=pltpu.CompilerParams(
            collective_id=0, has_side_effects=True, vmem_limit_bytes=63 * 1024 * 1024
        ),
        name="rl_step",
    )(estimate, views, kernel_x, kernel_y, kernel_z, offsets)
    return estimate * (1.0 + change)


def solution(mesh):
    in_specs = (P("depth", "tile", None), P(None, "depth", "tile", None), P(), P(), P(), P())
    return jax.shard_map(shards, mesh=mesh, in_specs=in_specs, out_specs=P("depth", "tile", None), check_vma=False)
```

```python
import jax
import jax.numpy as jnp
from jax import lax
from jax.experimental import pallas as pl
from jax.experimental.pallas import tpu as pltpu
from jax.sharding import PartitionSpec as P

MESH = pl.DeviceIdType.MESH
BF = jnp.bfloat16
F32 = jnp.float32
V = 8
T = 31
R = 32
H = 16
RH = R + 2 * H
NC = 1024
PAD = 128
CT = 256


def place(way, hop):
    if hop == 0:
        return 0, 0
    if hop == 8:
        return 0, 1
    return hop, way


GCOLS = ((0, 768), (768, 1024))
BTILES = ((0, 5), (5, 8))
STILES = ((0, 4), (4, 8))

SINGLY = ((0, 1), (7, 0), (7, 1))
DIAGONAL = ((0, 1),)


def body(
    est_in, views, kx_in, ky_in, kz_in, offs_in, out,
    est, kx, ky, kz, offs, obuf, share,
    gath, acc, blur, corr, back, amat, bmat, xfwd, xbwd, yfwd, ybwd, vbuf, part, own, sbuf, rbuf,
    g_send, g_recv, h_send, h_recv, in_sem, o_sem, y_send, y_recv, r_send, r_recv,
):
    b = lax.axis_index("depth")
    t = lax.axis_index("tile")
    nz = lax.axis_size("depth")
    nt = lax.axis_size("tile")
    rows_total = R * nt
    view_rows = 5 * rows_total // 8
    zr = lax.rem(b + 1, nz)
    zl = lax.rem(b + nz - 1, nz)
    tu = lax.rem(t + nt - 1, nt)
    td = lax.rem(t + 1, nt)
    z_to = ((t, zr), (t, zl))
    t_to = ((tu, b), (td, b))

    loads = [
        pltpu.make_async_copy(src, dst, in_sem.at[i])
        for i, (src, dst) in enumerate(
            ((est_in, est), (kx_in, kx), (ky_in, ky), (kz_in, kz), (offs_in, offs), (views, vbuf))
        )
    ]
    loads[0].start()
    barrier = pltpu.get_barrier_semaphore()
    corners = tuple((x, z) for x in (tu, td) for z in (zr, zl))
    for device in z_to + t_to + corners:
        pl.semaphore_signal(barrier, inc=1, device_id=device, device_id_type=MESH)
    for load in loads[1:]:
        load.start()

    def hop_copy(way, hop, q, k, c):
        pair, side = place(way, hop)
        pair2, side2 = place(way, hop + 1)
        rows = pl.ds(H + k * H, H) if c == 0 else pl.ds(H, R)
        cols = pl.ds(GCOLS[c][0], GCOLS[c][1] - GCOLS[c][0])
        sem = k if c == 0 else 2
        return pltpu.make_async_remote_copy(
            src_ref=gath.at[pair, side, q, rows, cols],
            dst_ref=gath.at[pair2, side2, q, rows, cols],
            send_sem=g_send.at[way, hop, q, sem],
            recv_sem=g_recv.at[way, hop, q, sem],
            device_id=z_to[way],
            device_id_type=MESH,
        )

    def halo_copy(pair, side, q, k, c):
        src, dst = ((H, H + R), (R, 0))[k]
        cols = pl.ds(GCOLS[c][0], GCOLS[c][1] - GCOLS[c][0])
        if (pair, side) in SINGLY:
            pair2, side2, device = pair, side, t_to[k]
            if (pair, side) in DIAGONAL:
                way = side if pair else 1 - q
                pair2, side2 = place(way, (pair or 8) - 1)
                device = ((tu, td)[k], (zr, zl)[way])
            source = gath.at[pair2, side2, q, pl.ds(src, H), cols]
            target = gath.at[pair, side, q, pl.ds(dst, H), cols]
        else:
            device = t_to[k]
            source = gath.at[pair, side, :, pl.ds(src, H), cols]
            target = gath.at[pair, side, :, pl.ds(dst, H), cols]
        return pltpu.make_async_remote_copy(
            src_ref=source,
            dst_ref=target,
            send_sem=h_send.at[pair, side, q, k, c],
            recv_sem=h_recv.at[pair, side, q, k, c],
            device_id=device,
            device_id_type=MESH,
        )

    def halo_copies(pair, side, c):
        qs = (0, 1) if (pair, side) in SINGLY else (0,)
        return [halo_copy(pair, side, q, k, c) for q in qs for k in range(2)]

    planes = ((1, 0), (0, 1))
    pieces = (((0, 0), (0, 1), (1, 0), (1, 1)), ((0, 0), (1, 0)))
    loads[0].wait()
    gath[0, 0, :, H : H + R, :] = est[...].astype(BF)
    pl.semaphore_wait(barrier, 8)
    for c in range(2):
        for i, k in pieces[c]:
            for way in range(2):
                hop_copy(way, 0, planes[way][i], k, c).start()
        for copy in halo_copies(0, 0, c):
            copy.start()
    for load in loads[1:5]:
        load.wait()

    lane = lax.broadcasted_iota(jnp.int32, (R, 2 * RH), 1)
    low = lane < RH
    src_row = jnp.where(low, lane, lane - RH)
    diff = src_row - lax.broadcasted_iota(jnp.int32, (R, 2 * RH), 0) - 1
    row_at = src_row + (t * R - H)
    exists = (row_at >= 0) & (row_at < rows_total)
    gap = lax.broadcasted_iota(jnp.int32, (PAD, PAD), 0) - lax.broadcasted_iota(jnp.int32, (PAD, PAD), 1)
    ring = jnp.where(gap + 15 < 0, gap + 15 + PAD, jnp.where(gap + 15 >= PAD, gap + 15 - PAD, gap + 15))

    def tables(v, carry):
        sx = kx[v, 0]
        sy = ky[v, 0]
        sz = kz[v, 0]
        for j in range(1, T):
            sx = sx + kx[v, j]
            sy = sy + ky[v, j]
            sz = sz + kz[v, j]
        xf = jnp.zeros((R, 2 * RH), F32)
        xb = jnp.zeros((R, 2 * RH), F32)
        cf = jnp.zeros((PAD, PAD), F32)
        cb = jnp.zeros((PAD, PAD), F32)
        for j in range(T):
            hit = diff == j
            xf = jnp.where(hit, kx[v, j], xf)
            xb = jnp.where(hit, kx[v, T - 1 - j], xb)
            hit = ring == j
            cf = jnp.where(hit, ky[v, j], cf)
            cb = jnp.where(hit, ky[v, T - 1 - j], cb)
        scale = jnp.full((R, 2 * RH), sx * sz, F32)
        xfwd[v] = jnp.where(exists, xf / scale, 0.0)
        xbwd[v] = jnp.where(exists, xb / scale, 0.0)
        for ref, c in ((yfwd, cf), (ybwd, cb)):
            c = c / jnp.full((PAD, PAD), sy, F32)
            bands = (
                jnp.where(gap >= PAD - 15, c, 0.0).astype(BF),
                jnp.where((gap <= 15) & (gap >= -15), c, 0.0).astype(BF),
                jnp.where(gap <= 15 - PAD, c, 0.0).astype(BF),
            )
            for i in range(3):
                ref[v, PAD * i : PAD * (i + 1), :] = bands[i]
        return carry

    lax.fori_loop(0, V, tables, 0)

    def mats(pair):
        offsets = (0, 8) if pair == 0 else (-pair, pair)
        zs = [2 * lax.rem(b + o + nz, nz) - 2 * b + 15 for o in offsets]

        def one(v, carry):
            xf = xfwd[v]
            xb = xbwd[v]
            c = {}
            for side in range(2):
                for q in range(2):
                    for p in range(2):
                        at = zs[side] + (q - p)
                        ok = (at >= 0) & (at < T)
                        c[side, q, p] = jnp.where(ok, kz[v, jnp.clip(at, 0, T - 1)], 0.0)
            for side in range(2):
                for p in range(2):
                    z = jnp.where(low, c[side, 0, p], c[side, 1, p])
                    amat[pair, pl.ds(pl.multiple_of(v * 64 + p * R, R), R), side * 128 : side * 128 + 128] = (xf * z).astype(BF)
                for q in range(2):
                    z = jnp.where(low, c[side, q, 0], c[side, q, 1])
                    first = side * 64 + q * R
                    bmat[pair, first : first + R, pl.ds(pl.multiple_of(v * 128, 128), 128)] = (xb * z).astype(BF)
            return carry

        lax.fori_loop(0, V, one, 0)

    def forward(pair, begin, end, chunk):
        def one(n, carry):
            cols = pl.ds(pl.multiple_of(n * CT, CT), CT)
            block = gath[pair, :, :, :, cols].reshape(4 * RH, CT)
            got = jnp.dot(amat[pair], block, preferred_element_type=F32)
            if not begin:
                got = got + acc[:, cols]
            if end:
                blur[:, pl.ds(pl.multiple_of(n * CT + PAD, PAD), CT)] = got.astype(BF)
            else:
                acc[:, cols] = got
            return carry

        lax.fori_loop(GCOLS[chunk][0] // CT, GCOLS[chunk][1] // CT, one, 0)

    blur[:, :PAD] = jnp.zeros((V * 64, PAD), BF)
    blur[:, PAD + NC :] = jnp.zeros((V * 64, PAD), BF)
    rid = lax.broadcasted_iota(jnp.int32, (R, 128), 0) + t * R
    seen_by = jnp.zeros((R, 128), F32)
    for v in range(V):
        seen_by = seen_by + jnp.where((rid >= offs[v]) & (rid < offs[v] + view_rows), 1.0, 0.0)
    share[...] = 1.0 / jnp.maximum(seen_by, 1.0)

    def halos(pair, c):
        for side in range(2):
            for copy in halo_copies(pair, side, c):
                copy.wait_recv()

    for hop in range(1, 8):
        for c in range(2):
            for i, k in pieces[c]:
                for way in range(2):
                    q = planes[way][i]
                    hop_copy(way, hop - 1, q, k, c).wait_recv()
                    if hop < 7 or i == 0:
                        hop_copy(way, hop, q, k, c).start()
                    for kk in (k,) if c == 0 else (0, 1):
                        if hop == 7 and i == 0:
                            halo_copy(0, 1, q, kk, c).start()
                        if hop == 7:
                            halo_copy(7, way, q, kk, c).start()
            if hop < 7:
                for side in range(2):
                    for copy in halo_copies(hop, side, c):
                        copy.start()
        mats(hop)
        if hop >= 2:
            for c in range(2):
                halos(hop - 1, c)
                forward(hop - 1, hop == 2, False, c)
    mats(0)
    loads[5].wait()

    row = lax.broadcasted_iota(jnp.int32, (2 * R, 128), 0)
    row = jnp.where(row >= R, row - R, row) + t * R

    def y_copy(v, k, c):
        src, dst = ((H, H + R), (R, 0))[k]
        cols = pl.ds(STILES[c][0] * 128, (STILES[c][1] - STILES[c][0]) * 128)
        return pltpu.make_async_remote_copy(
            src_ref=back.at[v, :, pl.ds(src, H), cols],
            dst_ref=back.at[v, :, pl.ds(dst, H), cols],
            send_sem=y_send.at[v, k, c],
            recv_sem=y_recv.at[v, k, c],
            device_id=t_to[k],
            device_id_type=MESH,
        )

    def view_work(v, c):
        inside = (row >= offs[v]) & (row < offs[v] + view_rows)
        rows = pl.ds(pl.multiple_of(v * 64, 64), 64)
        tiles = range(*BTILES[c])
        lhs = jnp.concatenate([blur[rows, n * 128 : n * 128 + 384] for n in tiles], axis=0)
        blurred = jnp.dot(lhs, yfwd[v], preferred_element_type=F32)
        none = jnp.zeros((2 * R, 128), BF)
        fixes = {-1: none, NC // 128: none}
        if c == 1:
            fixes[tiles[0] - 2] = corr[rows, :128]
            fixes[tiles[0] - 1] = corr[rows, 128:]
        for i, n in enumerate(tiles):
            seen = vbuf[v, :, :, n * 128 : (n + 1) * 128].astype(F32).reshape(2 * R, 128)
            ratio = seen / blurred[i * 64 : (i + 1) * 64]
            fixes[n] = jnp.where(inside, ratio - 1.0, 0.0).astype(BF)
        if c == 0:
            corr[rows, :128] = fixes[tiles[-1] - 1]
            corr[rows, 128:] = fixes[tiles[-1]]
        tiles = range(*STILES[c])
        lhs = jnp.concatenate([jnp.concatenate([fixes[n - 1], fixes[n], fixes[n + 1]], axis=1) for n in tiles], axis=0)
        spread = jnp.dot(lhs, ybwd[v], preferred_element_type=F32).astype(BF)
        for i, n in enumerate(tiles):
            back[v, :, H : H + R, n * 128 : (n + 1) * 128] = spread[i * 64 : (i + 1) * 64].reshape(2, R, 128)

    def view_step(c):
        def step(i, carry):
            for v in (2 * i, 2 * i + 1):
                view_work(v, c)
            for v in (2 * i, 2 * i + 1):
                for k in range(2):
                    y_copy(v, k, c).start()
            return carry

        lax.fori_loop(0, V // 2, step, 0)

    for c in range(2):
        halos(7, c)
        forward(7, False, False, c)
        for i, k in pieces[c]:
            if i == 0:
                for way in range(2):
                    hop_copy(way, 7, planes[way][0], k, c).wait_recv()
        halos(0, c)
        forward(0, False, True, c)
        view_step(c)

    def y_wait(c):
        def one(v, carry):
            for k in range(2):
                y_copy(v, k, c).wait_recv()
            return carry

        return one

    def sum_copy(way, step, c, i):
        tiles = pl.ds(17 * c + 9 * i, 9 - i)
        return pltpu.make_async_remote_copy(
            src_ref=sbuf.at[way, step, tiles],
            dst_ref=rbuf.at[way, step, tiles],
            send_sem=r_send.at[way, step, c, i],
            recv_sem=r_recv.at[way, step, c, i],
            device_id=z_to[way],
            device_id_type=MESH,
        )

    def project(pair, target, c, first, last):
        def one(n, carry):
            cols = pl.ds(pl.multiple_of(n * CT, CT), CT)
            block = back[first:last, :, :, cols].reshape((last - first) * 2 * RH, CT)
            got = jnp.dot(bmat[pair, :, first * 128 : last * 128], block, preferred_element_type=F32)
            if first:
                got = got + target[:, cols]
            target[:, cols] = got
            return carry

        lax.fori_loop(STILES[c][0] // 2, STILES[c][1] // 2, one, 0)

    spots = tuple((k, j) for k in range(2) for j in range(4))
    orders = ((0, 1), (1, 0))

    def message(source, way, step, c, i):
        q = orders[way][i]
        at = (64 if step == 0 else (1 - way) * 64) + q * R
        tiles = [source[at + k * H : at + (k + 1) * H, 128 * (4 * c + j) : 128 * (4 * c + j + 1)] for k, j in spots]
        first = 17 * c + 1 + 8 * i
        if step > 1 or (step == 1 and i == 0):
            sum_copy(way, step - 1, c, i).wait_recv()
            base = rbuf[way, step - 1, 17 * c].astype(F32)
            tiles = [tiles[n] + (rbuf[way, step - 1, first + n].astype(F32) + base) for n in range(8)]
        if i == 0:
            mean = sum(tiles[1:], tiles[0]) * 0.125
            sbuf[way, step, 17 * c] = mean.astype(BF)
        mean = sbuf[way, step, 17 * c].astype(F32)
        for n in range(8):
            sbuf[way, step, first + n] = (tiles[n] - mean).astype(BF)
        sum_copy(way, step, c, i).start()

    early = 6
    for c in range(2):
        if c == 0:
            lax.fori_loop(0, V, y_wait(c), 0)
            project(0, own, c, 0, V)
        else:
            lax.fori_loop(0, early, y_wait(c), 0)
            project(0, own, c, 0, early)
            lax.fori_loop(early, V, y_wait(c), 0)
            project(0, own, c, early, V)
        for way in range(2):
            message(own, way, 0, c, 0)
        project(7, part, c, 0, V)
    for step in range(1, 8):
        for c in range(2):
            for i in range(2):
                for way in range(2):
                    message(part, way, step, c, i)
            if step < 7:
                project(7 - step, part, c, 0, V)

    def result(c, q):
        cols = pl.ds(STILES[c][0] * 128, (STILES[c][1] - STILES[c][0]) * 128)
        return pltpu.make_async_copy(obuf.at[q, :, cols], out.at[q, :, cols], o_sem.at[c, q])

    for c in range(2):
        for way in range(2):
            for i in range(2):
                sum_copy(way, 7, c, i).wait_recv()
        for q in range(2):
            bases = [rbuf[way, 7, 17 * c].astype(F32) for way in range(2)]
            for n, (k, j) in enumerate(spots):
                rows = slice(k * H, (k + 1) * H)
                cols = slice(128 * (4 * c + j), 128 * (4 * c + j + 1))
                total = own[q * R + k * H : q * R + (k + 1) * H, cols]
                for way in range(2):
                    total = total + (rbuf[way, 7, 17 * c + 1 + 8 * orders[way].index(q) + n].astype(F32) + bases[way])
                obuf[q, rows, cols] = total * share[rows, :]
            result(c, q).start()

    for hop in range(8):
        for c in range(2):
            for way in range(2):
                for i, k in pieces[c]:
                    if hop < 7 or i == 0:
                        hop_copy(way, hop, planes[way][i], k, c).wait_send()
                for i in range(2):
                    if hop > 0 or i == 0:
                        sum_copy(way, hop, c, i).wait_send()
            for side in range(2):
                for copy in halo_copies(hop, side, c):
                    copy.wait_send()
    for c in range(2):
        for v in range(V):
            for k in range(2):
                y_copy(v, k, c).wait_send()
        for q in range(2):
            result(c, q).wait()


def shards(estimate, views, kernel_x, kernel_y, kernel_z, offsets):
    anywhere = pl.BlockSpec(memory_space=pl.ANY)
    dma = pltpu.SemaphoreType.DMA
    change = pl.pallas_call(
        body,
        out_shape=jax.ShapeDtypeStruct(estimate.shape, F32),
        in_specs=[anywhere] * 6,
        out_specs=anywhere,
        scratch_shapes=[
            pltpu.VMEM((2, R, NC), F32),
            pltpu.SMEM(kernel_x.shape, F32),
            pltpu.SMEM(kernel_y.shape, F32),
            pltpu.SMEM(kernel_z.shape, F32),
            pltpu.SMEM(offsets.shape, jnp.int32),
            pltpu.VMEM((2, R, NC), F32),
            pltpu.VMEM((R, 128), F32),
            pltpu.VMEM((8, 2, 2, RH, NC), BF),
            pltpu.VMEM((V * 64, NC), F32),
            pltpu.VMEM((V * 64, NC + 2 * PAD), BF),
            pltpu.VMEM((V * 64, 256), BF),
            pltpu.VMEM((V, 2, RH, NC), BF),
            pltpu.VMEM((8, V * 64, 256), BF),
            pltpu.VMEM((8, 128, V * 128), BF),
            pltpu.VMEM((V, R, 128), F32),
            pltpu.VMEM((V, R, 128), F32),
            pltpu.VMEM((V, 384, 128), BF),
            pltpu.VMEM((V, 384, 128), BF),
            pltpu.VMEM((V, 2, R, NC), BF),
            pltpu.VMEM((128, NC), F32),
            pltpu.VMEM((128, NC), F32),
            pltpu.VMEM((2, 8, 34, H, 128), BF),
            pltpu.VMEM((2, 8, 34, H, 128), BF),
            dma((2, 8, 2, 3)), dma((2, 8, 2, 3)),
            dma((8, 2, 2, 2, 2)), dma((8, 2, 2, 2, 2)),
            dma((6,)), dma((2, 2)),
            dma((V, 2, 2)), dma((V, 2, 2)),
            dma((2, 8, 2, 2)), dma((2, 8, 2, 2)),
        ],
        compiler_params=pltpu.CompilerParams(
            collective_id=0, has_side_effects=True, vmem_limit_bytes=63 * 1024 * 1024
        ),
        name="rl_step",
    )(estimate, views, kernel_x, kernel_y, kernel_z, offsets)
    return estimate * (1.0 + change)


def solution(mesh):
    in_specs = (P("depth", "tile", None), P(None, "depth", "tile", None), P(), P(), P(), P())
    return jax.shard_map(shards, mesh=mesh, in_specs=in_specs, out_specs=P("depth", "tile", None), check_vma=False)
```
